512 devices in a mesh: lat: 128 (over y, z, core), var: 4 (over x).
Axes of the slice: x: 4, y: 8, z: 8, core: 2. Of those that a mesh axis runs over, the one named last changes fastest.
Arguments:
- control: bfloat16 [4, 128, 64, 3072], P('var', 'lat'), may hold values from -6 to 6
- row_order: int32 [128], replicated, may hold values from 0 to 127, each once
- row_length: int32 [128], replicated, may hold values from 16 to 3072, as said below
- vertical: bfloat16 [4, 64, 64], P('var'), may hold values from -0.75 to 0.75
- amplitude: float32 [4, 768], P('var'), may hold values from 0.3 to 3
- meridional: bfloat16 [4, 128, 128], P('var'), may hold values from -16 to 16
- balance: bfloat16 [4, 64, 64], P('var'), may hold values from -0.75 to 0.75
Outputs:
- increment: bfloat16 [4, 128, 64, 3072], P('var', 'lat')
The draws below stay inside these ranges and needn't reach their ends.
Inputs may be any that keep to these rules, and one draw needn't show every extreme that they name: `row_length`: each a multiple of 4; the two middle latitude rows have exactly 3072 longitudes and the first and last rows 16.
All inputs are finite; a program needn't handle non-finite values.
Results may differ from the reference program's by a relative error of at most 0.0078.
Values may be sent and summed in bfloat16 or wider, within the bound.
A program may use at most 64 MiB of HBM per device.

```python
import math
import jax
import jax.numpy as jnp
from jax import lax

NLON = 3072
LEV = 64
WAVES = 768
VARS = 4
NLAT = 128


def draw_row_length(key, part):
    latitude = jnp.arange(NLAT, dtype=jnp.int32)
    halfway = NLAT // 2
    distance = jnp.minimum(latitude, NLAT - 1 - latitude)
    base_len = 16 + (NLON - 16) * distance // max(halfway - 1, 1)
    base_len = base_len // 4 * 4
    jitter = 4 * jax.random.randint(key, (NLAT,), 0, 4)
    lengths = jnp.maximum(base_len - jitter, 16)
    return jnp.where(distance == halfway - 1, NLON, lengths).astype(jnp.int32)


def draw_meridional(key, part):
    noise_key = jax.random.fold_in(key, 11)
    position = jnp.arange(NLAT).astype(jnp.float32)
    spread = (position[:, None] - position[None, :]) / (NLAT / 3.0)
    envelope = jnp.exp(-spread * spread)
    noise = jnp.clip(jax.random.normal(noise_key, (VARS, NLAT, NLAT), jnp.float32), -3.0, 3.0)
    matrix = jnp.eye(NLAT, dtype=jnp.float32)[None] + noise * envelope[None] * (2.0 / math.sqrt(NLAT))
    return matrix.astype(jnp.bfloat16)


def block_scale(rng, dims, split, smallest, top_value):
    def one(dim, blocks):
        heights = jax.random.uniform(jax.random.fold_in(jax.random.fold_in(rng, 6), dim), (blocks,), jnp.float32, smallest / len(split), top_value / len(split))
        return jnp.repeat(jnp.exp(heights), dims[dim] // blocks).reshape((-1,) + (1,) * (len(dims) - dim - 1))

    gain = one(*split[0])
    for cut in split[1:]:
        gain = gain * one(*cut)
    return gain


def bell_draw(key, extent, deviation, bound, pieces=(), held_as=jnp.bfloat16):
    level = block_scale(key, extent, pieces, -0.22, 0.18) if pieces else 1.0
    entries = jax.random.normal(key, extent, jnp.float32) * deviation * level
    return jnp.minimum(jnp.maximum(entries, -bound), bound).astype(held_as)


def setup_inputs(seed: int = 0) -> dict:
    splits = jax.random.split(jax.random.key(seed), 8)
    return {
        "control": bell_draw(splits[0], (VARS, NLAT, LEV, NLON), 1.0, 6.0, ((0, 4), (1, 128))),
        "row_order": jax.random.permutation(splits[1], NLAT).astype(jnp.int32),
        "row_length": draw_row_length(jax.random.fold_in(splits[7], 71), 0),
        "vertical": bell_draw(splits[3], (VARS, LEV, LEV), LEV ** -0.5, 0.75, ((0, 4),)),
        "amplitude": jnp.clip(jnp.exp(math.log(3.0) - 2.3025851 * jax.random.uniform(splits[4], (VARS, WAVES), jnp.float32) ** block_scale(splits[4], (VARS, WAVES), ((0, 4),), -0.2, 0.2)), 0.3, 3.0),
        "meridional": draw_meridional(jax.random.fold_in(splits[7], 71), 0),
        "balance": bell_draw(splits[6], (VARS, LEV, LEV), LEV ** -0.5, 0.75, ((0, 4),)),
    }


def zonal_basis(lengths, offset, width, waves):
    columns = offset + jnp.arange(width, dtype=jnp.int32)
    wavenum = jnp.arange(waves, dtype=jnp.int32)
    period = lengths.astype(jnp.int32)[:, None, None]
    phases = (columns[None, :, None] * wavenum[None, None, :]) % period
    angles = (2.0 * math.pi) * phases.astype(jnp.float32) / period.astype(jnp.float32)
    inside = (columns[None, :, None] < period) & (wavenum[None, None, :] <= (period - 1) // 2)
    cosine = jnp.where(inside, jnp.cos(angles), 0.0)
    sines = jnp.where(inside, jnp.sin(angles), 0.0)
    return jnp.concatenate([cosine, sines], axis=2)


def wave_scaling(lengths, waves):
    wavenum = jnp.arange(waves, dtype=jnp.int32)
    factor = jnp.where(wavenum == 0, 1.0, 2.0).astype(jnp.float32)
    factor = jnp.concatenate([factor, factor])
    return factor[None, :] / lengths.astype(jnp.float32)[:, None]


def reference(control, row_order, row_length, vertical, amplitude, meridional, balance):
    lat_total = control.shape[1]
    lon_count = control.shape[3]
    waves = amplitude.shape[1]
    slot_len = row_length[row_order]
    amp_both = jnp.concatenate([amplitude, amplitude], axis=1)
    vert_float = vertical.astype(jnp.float32)

    def analyse(inputs_row):
        fields, length = inputs_row
        lengths = length[None]
        basis_tab = zonal_basis(lengths, 0, lon_count, waves)
        analysis_tab = (basis_tab * wave_scaling(lengths, waves)[:, None, :]).astype(jnp.bfloat16)[0]
        levels = jnp.einsum('vml,vlj->vmj', vert_float, fields.astype(jnp.float32)).astype(jnp.bfloat16)
        summed = jnp.einsum('vmj,jc->vmc', levels.astype(jnp.float32), analysis_tab.astype(jnp.float32))
        return (summed * amp_both[:, None, :]).astype(jnp.bfloat16)

    coeffs = lax.map(analyse, (jnp.moveaxis(control, 1, 0), slot_len))
    blended = []
    for var_idx in range(VARS):
        slot_mat = meridional[var_idx][row_order][:, row_order].astype(jnp.float32)
        flattened = coeffs[:, var_idx].reshape(lat_total, -1).astype(jnp.float32)
        product = jnp.dot(slot_mat, flattened, preferred_element_type=jnp.float32).astype(jnp.bfloat16)
        blended.append(product.reshape(lat_total, coeffs.shape[2], coeffs.shape[3]))
    balanced = [blended[0]]
    for var_idx in range(1, VARS):
        lifted = jnp.einsum('ml,plc->pmc', balance[var_idx].astype(jnp.float32), blended[0].astype(jnp.float32))
        balanced.append((blended[var_idx].astype(jnp.float32) + lifted).astype(jnp.bfloat16))
    stacked = jnp.stack(balanced, axis=1)

    def synthesise(inputs_row):
        spectra, length = inputs_row
        basis_tab = zonal_basis(length[None], 0, lon_count, waves)[0].astype(jnp.bfloat16)
        return jnp.einsum('vmc,jc->vmj', spectra.astype(jnp.float32), basis_tab.astype(jnp.float32)).astype(jnp.bfloat16)

    output = lax.map(synthesise, (stacked, slot_len))
    return jnp.moveaxis(output, 0, 1)
```

```python
import functools
import math

import jax
import jax.numpy as jnp
from jax import lax
from jax.experimental import pallas as pl
from jax.experimental.pallas import tpu as pltpu
from jax.sharding import PartitionSpec as P

LANES = 128
SUBS = 8
F32 = jnp.float32
BF16 = jnp.bfloat16
MESH = pl.DeviceIdType.MESH


def iota(shape, dim):
    return lax.broadcasted_iota(jnp.int32, shape, dim)


def nt_dot(a, b):
    return lax.dot_general(a, b, (((1,), (1,)), ((), ())), preferred_element_type=F32)


def own_length(order_ref, length_ref):
    return length_ref[order_ref[lax.axis_index("lat")]]


def wave_seeds(period, cos_ref, sin_ref, groups, per_peer):
    shape = cos_ref.shape
    row = iota(shape, 0)
    local = row - groups
    fine = 4 * (local % SUBS) + local // SUBS
    wave = jnp.where(row < groups, 4 * per_peer * row, fine).astype(F32)
    phase = wave * iota(shape, 1).astype(F32)
    inverse = 1.0 / period
    phase = phase - jnp.floor(phase * inverse + 0.5) * period
    quadrant = jnp.floor(phase * (4.0 * inverse) + 0.5)
    angle = (4.0 * phase - quadrant * period) * inverse * (0.5 * math.pi)
    sq = angle * angle
    sine = angle * (1.0 + sq * (-1.0 / 6 + sq * (1.0 / 120 + sq * (-1.0 / 5040 + sq * (1.0 / 362880)))))
    cosine = 1.0 + sq * (-0.5 + sq * (1.0 / 24 + sq * (-1.0 / 720 + sq * (1.0 / 40320))))
    odd = jnp.abs(quadrant) == 1.0
    flip = jnp.abs(quadrant) == 2.0
    sign = jnp.where(flip, -1.0, jnp.where(odd, quadrant, 1.0))
    cos_ref[...] = jnp.where(odd, -sign * sine, sign * cosine)
    sin_ref[...] = jnp.where(odd, sign * cosine, sign * sine)


def fill_table(cos_ref, sin_ref, table_ref, groups, quarter):
    rows = groups * SUBS
    blocks = quarter // LANES

    def one(step, carry):
        rem = step // blocks
        start = pl.multiple_of(step % blocks * LANES, LANES)
        cols = pl.ds(start, LANES)
        fine = pl.ds(pl.multiple_of(groups + rem * SUBS, SUBS), SUBS)
        cos_c = cos_ref[pl.ds(0, groups), cols][:, None, :]
        sin_c = sin_ref[pl.ds(0, groups), cols][:, None, :]
        cos_f = cos_ref[fine, cols][None, :, :]
        sin_f = sin_ref[fine, cols][None, :, :]
        cosine = cos_c * cos_f - sin_c * sin_f
        sine = sin_c * cos_f + cos_c * sin_f
        dest = pl.ds(pl.multiple_of(rem * rows, rows), rows)
        table_ref[dest, cols] = cosine.reshape(rows, LANES).astype(BF16)
        table_ref[dest, pl.ds(pl.multiple_of(start + quarter, LANES), LANES)] = sine.reshape(
            rows, LANES
        ).astype(BF16)
        return carry

    lax.fori_loop(0, 4 * blocks, one, 0)


def row_wave(lat_total, per_peer):
    groups = lat_total // 4
    shape = (lat_total, SUBS, LANES)
    peer = iota(shape, 0)
    sub = iota(shape, 1)
    wave = 4 * (peer % groups * per_peer + sub) + peer // groups
    return wave, sub < per_peer


def analysis_kernel(
    order_ref, length_ref, control_ref, vertical_ref, coeff_ref, cos_ref, sin_ref, table_ref, level_ref
):
    lat_total, per_peer = coeff_ref.shape[0], coeff_ref.shape[1]
    groups = lat_total // 4
    rows = groups * SUBS
    lons = control_ref.shape[-1]
    quarter = lons // 4
    blocks = quarter // LANES
    length = own_length(order_ref, length_ref)
    period = length.astype(F32)
    wave_seeds(period, cos_ref, sin_ref, groups, per_peer)
    fill_table(cos_ref, sin_ref, table_ref, groups, quarter)
    levels = jnp.dot(vertical_ref[0], control_ref[0, 0], preferred_element_type=F32)
    level_ref[:, pl.ds(0, lons)] = levels.astype(BF16).astype(F32)
    count = levels.shape[0]
    step = length // 4
    lane = iota((count, LANES), 1)

    def shifted(part):
        base = part * step
        start = base // LANES
        shift = base % LANES
        back = (LANES - shift) % LANES
        pieces = []
        rolled = [
            pltpu.roll(
                level_ref[:, pl.ds(pl.multiple_of((start + b) * LANES, LANES), LANES)], back, 1
            )
            for b in range(blocks + 1)
        ]
        for b in range(blocks):
            both = jnp.where(lane < LANES - shift, rolled[b], rolled[b + 1])
            pieces.append(jnp.where(lane + b * LANES < step, both, 0.0))
        return jnp.concatenate(pieces, axis=1)

    x0, x1, x2, x3 = (shifted(q) for q in range(4))
    y0 = ((x0 + x2) + (x1 + x3)).astype(BF16)
    y2 = ((x0 + x2) - (x1 + x3)).astype(BF16)
    a = (x0 - x2).astype(BF16)
    b = (x1 - x3).astype(BF16)
    zero = jnp.zeros_like(y0)
    weights = (
        ((y0, zero), (zero, y0)),
        ((a, -b), (b, a)),
        ((y2, zero), (zero, y2)),
        ((a, b), (-b, a)),
    )
    wave, held = row_wave(lat_total, per_peer)
    scale = jnp.where(wave == 0, 1.0, 2.0) / period
    scale = jnp.where(held & (wave <= (length - 1) // 2), scale, 0.0)
    for rem in range(4):
        upper, lower = weights[rem]
        mixed = jnp.concatenate(
            [jnp.concatenate(upper, axis=1), jnp.concatenate(lower, axis=1)], axis=0
        )
        part = nt_dot(table_ref[pl.ds(rem * rows, rows), :], mixed)
        part = part.reshape(groups, SUBS, LANES) * scale[rem * groups : (rem + 1) * groups]
        coeff_ref[pl.ds(rem * groups, groups)] = part[:, :per_peer, :].astype(BF16)


def synthesis_kernel(
    order_ref, length_ref, balanced_ref, out_ref, cos_ref, sin_ref, table_ref, spec_ref, wide_ref
):
    lat_total, per_peer = balanced_ref.shape[0], balanced_ref.shape[1]
    groups = lat_total // 4
    rows = groups * SUBS
    count, lons = out_ref.shape[-2], out_ref.shape[-1]
    quarter = lons // 4
    blocks = quarter // LANES
    length = own_length(order_ref, length_ref)
    period = length.astype(F32)
    wave_seeds(period, cos_ref, sin_ref, groups, per_peer)
    fill_table(cos_ref, sin_ref, table_ref, groups, quarter)
    wave, _ = row_wave(lat_total, per_peer)
    spec_ref[...] = jnp.zeros_like(spec_ref)
    spec_ref[:, pl.ds(0, per_peer), :] = jnp.where(
        wave[:, :per_peer] <= (length - 1) // 2, balanced_ref[...].astype(F32), 0.0
    )
    turned = spec_ref[...].reshape(lat_total * SUBS, LANES).T.astype(BF16)

    def parts(rem):
        both = turned[:, rem * rows : (rem + 1) * rows]
        return both[:count], both[count:]

    def against(rem, on_cos, on_sin):
        here = pl.ds(rem * rows, rows)
        return jnp.dot(
            on_cos, table_ref[here, pl.ds(0, quarter)], preferred_element_type=F32
        ) + jnp.dot(on_sin, table_ref[here, pl.ds(quarter, quarter)], preferred_element_type=F32)

    c0, s0 = parts(0)
    c1, s1 = parts(1)
    c2, s2 = parts(2)
    c3, s3 = parts(3)
    e0 = against(0, c0, s0)
    e2 = against(2, c2, s2)
    ab = against(
        1, jnp.concatenate([c1, s1], axis=0), jnp.concatenate([s1, -c1], axis=0)
    ) + against(3, jnp.concatenate([c3, -s3], axis=0), jnp.concatenate([s3, c3], axis=0))
    a, b = ab[:count], ab[count:]
    step = length // 4
    lane = iota((count, LANES), 1)
    wide_ref[...] = jnp.zeros_like(wide_ref)
    for part, piece in enumerate(((e0 + e2) + a, (e0 - e2) + b, (e0 + e2) - a, (e0 - e2) - b)):
        base = part * step
        start = base // LANES
        shift = base % LANES
        before = jnp.zeros((count, LANES), F32)
        for blk in range(blocks + 1):
            if blk < blocks:
                own = piece[:, blk * LANES : (blk + 1) * LANES]
                own = jnp.where(lane + blk * LANES < step, own, 0.0)
                rolled = pltpu.roll(own, shift, 1)
            else:
                rolled = jnp.zeros((count, LANES), F32)
            here = pl.ds(pl.multiple_of((start + blk) * LANES, LANES), LANES)
            wide_ref[:, here] += jnp.where(lane >= shift, rolled, before)
            before = rolled
    out_ref[0, 0] = wide_ref[:, pl.ds(0, lons)].astype(BF16)


def blend_kernel(
    order_ref,
    amp_ref,
    coeff_ref,
    meridional_ref,
    balance_ref,
    balanced_ref,
    recv_ref,
    mixed_ref,
    wide_ref,
    root_ref,
    root_out_ref,
    send_sem,
    recv_sem,
    local_sem,
    root_send_sem,
    root_recv_sem,
    back_send_sem,
    back_recv_sem,
):
    lat_total, per_peer = coeff_ref.shape[0], coeff_ref.shape[1]
    groups = lat_total // 4
    me = lax.axis_index("lat")
    var = lax.axis_index("var")
    var_total = lax.axis_size("var")

    def peer_at(step):
        return (me + step * 37) % lat_total

    barrier = pltpu.get_barrier_semaphore()

    def greet(step, carry):
        pl.semaphore_signal(barrier, 1, device_id={"lat": peer_at(step)}, device_id_type=MESH)
        return carry

    lax.fori_loop(1, lat_total, greet, 0)
    for other in range(1, var_total):
        pl.semaphore_signal(
            barrier, 1, device_id={"var": (var + other) % var_total}, device_id_type=MESH
        )
    pick = jnp.where(iota((lat_total, lat_total), 0) == order_ref[...], 1.0, 0.0).astype(BF16)
    slot_mat = jnp.dot(meridional_ref[0], pick, preferred_element_type=F32).astype(BF16)
    slot_mat = lax.dot_general(
        pick, slot_mat, (((0,), (0,)), ((), ())), preferred_element_type=F32
    ).astype(BF16)
    block = balance_ref[0]
    none = jnp.zeros_like(block)
    lift = jnp.concatenate(
        [jnp.concatenate([block, none], axis=1), jnp.concatenate([none, block], axis=1)], axis=0
    )
    pl.semaphore_wait(barrier, lat_total - 1 + var_total - 1)

    def exchange(src_ref, dst_ref, src_sem, dst_sem):
        def send(step, carry):
            peer = peer_at(step)
            pltpu.make_async_remote_copy(
                src_ref=src_ref.at[peer],
                dst_ref=dst_ref.at[me],
                send_sem=src_sem,
                recv_sem=dst_sem,
                device_id={"lat": peer},
                device_id_type=MESH,
            ).start()
            return carry

        lax.fori_loop(1, lat_total, send, 0)
        own = pltpu.make_async_copy(src_ref.at[me], dst_ref.at[me], local_sem)
        own.start()
        own.wait()
        rest = pl.ds(0, lat_total - 1)
        pltpu.make_async_copy(src_ref.at[rest], src_ref.at[rest], src_sem).wait()
        pltpu.make_async_copy(dst_ref.at[rest], dst_ref.at[rest], dst_sem).wait()

    exchange(coeff_ref, recv_ref, send_sem, recv_sem)
    wide_ref[:, pl.ds(0, per_peer), :] = recv_ref[...].astype(F32)
    for sub in range(per_peer):
        row = wide_ref[:, sub, :].astype(BF16)
        wave = 4 * (me % groups * per_peer + sub) + me // groups
        product = jnp.dot(slot_mat, row, preferred_element_type=F32) * amp_ref[0, wave]
        wide_ref[:, sub, :] = product
    blended = wide_ref[...]

    @pl.when(var == 0)
    def _():
        rounded = blended[:, :per_peer, :].astype(BF16)
        mixed_ref[...] = rounded
        root_out_ref[...] = rounded
        copies = []
        for other in (2, 1, 3):
            if other < var_total:
                copies.append(
                    pltpu.make_async_remote_copy(
                        src_ref=root_out_ref,
                        dst_ref=root_ref,
                        send_sem=root_send_sem.at[other],
                        recv_sem=root_recv_sem,
                        device_id={"var": other},
                        device_id_type=MESH,
                    )
                )
        for copy in copies:
            copy.start()
        for copy in copies:
            copy.wait_send()

    @pl.when(var > 0)
    def _():
        pltpu.make_async_copy(root_ref, root_ref, root_recv_sem).wait()
        wide_ref[:, pl.ds(0, per_peer), :] = root_ref[...].astype(F32)
        root = wide_ref[...].reshape(lat_total * SUBS, LANES).astype(BF16)
        lifted = nt_dot(root, lift).reshape(lat_total, SUBS, LANES)
        mixed_ref[...] = (blended + lifted)[:, :per_peer, :].astype(BF16)

    exchange(mixed_ref, balanced_ref, back_send_sem, back_recv_sem)


def body(control, row_order, row_length, vertical, amplitude, meridional, balance):
    lat_total = row_order.shape[0]
    levels, lons = control.shape[2:]
    waves = amplitude.shape[1]
    per_peer = waves // lat_total
    groups = lat_total // 4
    quarter = lons // 4
    vmem = pl.BlockSpec(memory_space=pltpu.VMEM)
    smem = pl.BlockSpec(memory_space=pltpu.SMEM)
    packed = jax.ShapeDtypeStruct((lat_total, per_peer, LANES), BF16)
    seeds = pltpu.VMEM((groups + 4 * SUBS, quarter), F32)
    table = pltpu.VMEM((lat_total * SUBS, 2 * quarter), BF16)
    coeffs = pl.pallas_call(
        analysis_kernel,
        name="analysis",
        out_shape=packed,
        in_specs=[smem, smem, vmem, vmem],
        out_specs=vmem,
        scratch_shapes=[seeds, seeds, table, pltpu.VMEM((levels, lons + LANES), F32)],
    )(row_order, row_length, control, vertical)
    wide = pltpu.VMEM((lat_total, SUBS, LANES), F32)
    block = pltpu.VMEM(packed.shape, BF16)
    dma = pltpu.SemaphoreType.DMA
    balanced = pl.pallas_call(
        blend_kernel,
        name="blend",
        out_shape=packed,
        in_specs=[vmem, smem, vmem, vmem, vmem],
        out_specs=vmem,
        scratch_shapes=[
            block,
            block,
            wide,
            block,
            block,
            dma(()),
            dma(()),
            dma(()),
            dma((4,)),
            dma(()),
            dma(()),
            dma(()),
        ],
        compiler_params=pltpu.CompilerParams(collective_id=0, has_side_effects=True),
    )(row_order.reshape(1, lat_total), amplitude, coeffs, meridional, balance)
    return pl.pallas_call(
        synthesis_kernel,
        name="synthesis",
        out_shape=jax.ShapeDtypeStruct(control.shape, BF16),
        in_specs=[smem, smem, vmem],
        out_specs=vmem,
        scratch_shapes=[seeds, seeds, table, wide, pltpu.VMEM((levels, lons + LANES), F32)],
    )(row_order, row_length, balanced)


def solution(mesh):
    return jax.shard_map(
        body,
        mesh=mesh,
        in_specs=(
            P("var", "lat", None, None),
            P(),
            P(),
            P("var", None, None),
            P("var", None),
            P("var", None, None),
            P("var", None, None),
        ),
        out_specs=P("var", "lat", None, None),
        check_vma=False,
    )
```

```python
import functools
import math

import jax
import jax.numpy as jnp
from jax import lax
from jax.experimental import pallas as pl
from jax.experimental.pallas import tpu as pltpu
from jax.sharding import PartitionSpec as P

LANES = 128
SUBS = 8
ROW = 16
F32 = jnp.float32
BF16 = jnp.bfloat16
MESH = pl.DeviceIdType.MESH


def iota(shape, dim):
    return lax.broadcasted_iota(jnp.int32, shape, dim)


def nt_dot(a, b):
    return lax.dot_general(a, b, (((1,), (1,)), ((), ())), preferred_element_type=F32)


def own_length(order_ref, length_ref):
    return length_ref[order_ref[lax.axis_index("lat")]]


def wave_seeds(period, cos_ref, sin_ref, groups, per_peer):
    shape = cos_ref.shape
    row = iota(shape, 0)
    local = row - groups
    fine = 4 * (local % SUBS) + local // SUBS
    wave = jnp.where(row < groups, 4 * per_peer * row, fine).astype(F32)
    phase = wave * iota(shape, 1).astype(F32)
    inverse = 1.0 / period
    phase = phase - jnp.floor(phase * inverse + 0.5) * period
    quadrant = jnp.floor(phase * (4.0 * inverse) + 0.5)
    angle = (4.0 * phase - quadrant * period) * inverse * (0.5 * math.pi)
    sq = angle * angle
    sine = angle * (1.0 + sq * (-1.0 / 6 + sq * (1.0 / 120 + sq * (-1.0 / 5040 + sq * (1.0 / 362880)))))
    cosine = 1.0 + sq * (-0.5 + sq * (1.0 / 24 + sq * (-1.0 / 720 + sq * (1.0 / 40320))))
    odd = jnp.abs(quadrant) == 1.0
    flip = jnp.abs(quadrant) == 2.0
    sign = jnp.where(flip, -1.0, jnp.where(odd, quadrant, 1.0))
    cos_ref[...] = jnp.where(odd, -sign * sine, sign * cosine)
    sin_ref[...] = jnp.where(odd, sign * cosine, sign * sine)


def fill_table(cos_ref, sin_ref, table_ref, groups):
    blocks = table_ref.shape[0] // 2
    rows = groups * SUBS

    def one(step, carry):
        rem, blk = step // blocks, step % blocks
        cols = pl.ds(pl.multiple_of(blk * LANES, LANES), LANES)
        fine = pl.ds(pl.multiple_of(groups + rem * SUBS, SUBS), SUBS)
        cos_f, sin_f = cos_ref[fine, cols], sin_ref[fine, cols]
        for group in range(0, groups, 2):
            cosine, sine = [], []
            for g in (group, group + 1):
                cos_c, sin_c = cos_ref[pl.ds(g, 1), cols], sin_ref[pl.ds(g, 1), cols]
                cosine.append(cos_c * cos_f - sin_c * sin_f)
                sine.append(sin_c * cos_f + cos_c * sin_f)
            dest = pl.ds(pl.multiple_of(rem * rows + group * SUBS, 2 * SUBS), 2 * SUBS)
            table_ref[blk, dest, :] = jnp.concatenate(cosine, axis=0).astype(BF16)
            table_ref[blk + blocks, dest, :] = jnp.concatenate(sine, axis=0).astype(BF16)
        return carry

    lax.fori_loop(0, 4 * blocks, one, 0)


def table_rows(table_ref, rem, rows, first, last):
    here = pl.ds(rem * rows, rows)
    return jnp.concatenate([table_ref[b, here, :] for b in range(first, last)], axis=1)


def row_wave(lat_total, per_peer):
    groups = lat_total // 4
    shape = (lat_total, SUBS, LANES)
    peer = iota(shape, 0)
    sub = iota(shape, 1)
    wave = 4 * (peer % groups * per_peer + sub) + peer // groups
    return wave, sub < per_peer


def analyse(length, per_peer, control_ref, vertical_ref, coeff_ref, table_ref, level_ref):
    lat_total = coeff_ref.shape[0]
    groups = lat_total // 4
    rows = groups * SUBS
    lons = control_ref.shape[-1]
    quarter = lons // 4
    blocks = quarter // LANES
    period = length.astype(F32)
    levels = jnp.dot(vertical_ref[0], control_ref[0, 0], preferred_element_type=F32)
    level_ref[:, pl.ds(0, lons)] = levels.astype(BF16)
    level_ref[:, pl.ds(lons, LANES)] = jnp.zeros((levels.shape[0], LANES), BF16)
    count = levels.shape[0]
    step = length // 4
    lane = iota((count, LANES), 1)
    columns = [level_ref[:, pl.ds(b * LANES, LANES)] for b in range(4 * blocks + 1)]

    def shifted(part):
        base = part * step
        start, shift = base // LANES, base % LANES
        held = columns
        bit = 1 << max(part * blocks, 1).bit_length() - 1
        while bit and part:
            moved = [held[c + bit] if c + bit < len(held) else held[c] for c in range(len(held))]
            set_here = start // bit % 2 == 1
            held = [jnp.where(set_here, m, h) for m, h in zip(moved, held)]
            held = held[: blocks + bit]
            bit //= 2
        pairs = [jnp.concatenate([held[b], held[b + 1]], axis=1) for b in range(blocks)]
        if part:
            turn = (2 * LANES, LANES)
            place = jnp.where(iota(turn, 0) == iota(turn, 1) + shift, 1.0, 0.0).astype(BF16)
            both = jnp.dot(jnp.concatenate(pairs, axis=0), place, preferred_element_type=F32)
            parts = [both[b * count : (b + 1) * count] for b in range(blocks)]
        else:
            parts = [held[b].astype(F32) for b in range(blocks)]
        return jnp.concatenate(
            [jnp.where(lane + b * LANES < step, parts[b], 0.0) for b in range(blocks)], axis=1
        )

    x0, x1, x2, x3 = (shifted(q) for q in range(4))
    y0 = ((x0 + x2) + (x1 + x3)).astype(BF16)
    y2 = ((x0 + x2) - (x1 + x3)).astype(BF16)
    a = (x0 - x2).astype(BF16)
    b = (x1 - x3).astype(BF16)
    zero = jnp.zeros_like(y0)
    weights = (
        ((y0, zero), (zero, y0)),
        ((a, -b), (b, a)),
        ((y2, zero), (zero, y2)),
        ((a, b), (-b, a)),
    )
    wave, held = row_wave(lat_total, per_peer)
    scale = jnp.where(wave == 0, 1.0, 2.0) / period
    scale = jnp.where(held & (wave <= (length - 1) // 2), scale, 0.0)
    for rem in range(4):
        upper, lower = weights[rem]
        mixed = jnp.concatenate(
            [jnp.concatenate(upper, axis=1), jnp.concatenate(lower, axis=1)], axis=0
        )
        part = nt_dot(table_rows(table_ref, rem, rows, 0, 2 * blocks), mixed)
        part = part.reshape(groups, SUBS, LANES) * scale[rem * groups : (rem + 1) * groups]
        coeff_ref[pl.ds(rem * groups, groups)] = part.astype(BF16)


def synthesis_kernel(
    per_peer, order_ref, length_ref, balanced_ref, table_hbm, out_ref, table_ref, wide_ref, sems
):
    lat_total = balanced_ref.shape[0]
    groups = lat_total // 4
    rows = groups * SUBS
    count, lons = out_ref.shape[-2], out_ref.shape[-1]
    quarter = lons // 4
    blocks = quarter // LANES
    length = own_length(order_ref, length_ref)
    loads = []
    for rem in range(4):
        here = pl.ds(rem * rows, rows)
        loads.append(
            pltpu.make_async_copy(table_hbm.at[:, here], table_ref.at[:, here], sems.at[rem])
        )
        loads[-1].start()
    wide_ref[...] = jnp.zeros_like(wide_ref)
    wave, held = row_wave(lat_total, per_peer)
    spectra = jnp.where(
        held & (wave <= (length - 1) // 2), balanced_ref[...].astype(F32), 0.0
    )
    turned = spectra.reshape(lat_total * SUBS, LANES).T.astype(BF16)

    def parts(rem):
        both = turned[:, rem * rows : (rem + 1) * rows]
        return both[:count], both[count:]

    def against(rem, on_cos, on_sin):
        loads[rem].wait()
        return jnp.dot(
            on_cos, table_rows(table_ref, rem, rows, 0, blocks), preferred_element_type=F32
        ) + jnp.dot(
            on_sin, table_rows(table_ref, rem, rows, blocks, 2 * blocks), preferred_element_type=F32
        )

    c0, s0 = parts(0)
    c1, s1 = parts(1)
    c2, s2 = parts(2)
    c3, s3 = parts(3)
    e0 = against(0, c0, s0)
    e2 = against(2, c2, s2)
    ab = against(
        1, jnp.concatenate([c1, s1], axis=0), jnp.concatenate([s1, -c1], axis=0)
    ) + against(3, jnp.concatenate([c3, -s3], axis=0), jnp.concatenate([s3, c3], axis=0))
    a, b = ab[:count], ab[count:]
    step = length // 4
    lane = iota((count, LANES), 1)
    for part, piece in enumerate(((e0 + e2) + a, (e0 - e2) + b, (e0 + e2) - a, (e0 - e2) - b)):
        base = part * step
        start = base // LANES
        shift = base % LANES
        before = jnp.zeros((count, LANES), F32)
        for blk in range(blocks + 1):
            if blk < blocks:
                own = piece[:, blk * LANES : (blk + 1) * LANES]
                own = jnp.where(lane + blk * LANES < step, own, 0.0)
                rolled = pltpu.roll(own, shift, 1)
            else:
                rolled = jnp.zeros((count, LANES), F32)
            here = pl.ds(pl.multiple_of((start + blk) * LANES, LANES), LANES)
            wide_ref[:, here] += jnp.where(lane >= shift, rolled, before)
            before = rolled
    out_ref[0, 0] = wide_ref[:, pl.ds(0, lons)].astype(BF16)


def blend_kernel(
    per_peer,
    order_smem,
    length_ref,
    amp_ref,
    order_ref,
    control_ref,
    vertical_ref,
    meridional_ref,
    balance_ref,
    balanced_ref,
    table_hbm,
    cos_ref,
    sin_ref,
    table_ref,
    level_ref,
    coeff_ref,
    recv_ref,
    wide_ref,
    product_ref,
    root_ref,
    mixed_ref,
    line_sem,
    table_sem,
    local_sem,
    send_sem,
    recv_sem,
    root_send_sem,
    root_recv_sem,
    back_send_sem,
    back_recv_sem,
):
    lat_total = balanced_ref.shape[0]
    groups = lat_total // 4
    me = lax.axis_index("lat")
    var = lax.axis_index("var")
    var_total = lax.axis_size("var")
    row_size = ROW if lat_total % ROW == 0 else 2
    columns = lat_total // row_size
    chips = row_size // 2
    core, spot, line = me % 2, me // 2 % chips, me // row_size
    barrier = pltpu.get_barrier_semaphore()

    def greet(sem, **where):
        pl.semaphore_signal(sem, 1, device_id=where, device_id_type=MESH)

    def greet_column(sem):
        for step in range(1, columns):
            greet(sem, lat=(line + step) % columns * row_size + me % row_size)

    for step in range(1, row_size):
        greet(barrier, lat=line * row_size + (me + step) % row_size)
    greet_column(barrier)
    for step in range(1, var_total):
        greet(barrier, var=(var + step) % var_total)

    length = own_length(order_smem, length_ref)
    wave_seeds(length.astype(F32), cos_ref, sin_ref, groups, per_peer)
    fill_table(cos_ref, sin_ref, table_ref, groups)
    table_copy = pltpu.make_async_copy(table_ref, table_hbm, table_sem)
    table_copy.start()
    pl.semaphore_wait(barrier, row_size - 1 + columns - 1 + var_total - 1)
    greet_column(line_sem)
    analyse(length, per_peer, control_ref, vertical_ref, coeff_ref, table_ref, level_ref)
    pl.semaphore_wait(line_sem, columns - 1)

    def to_peer(src_ref, dst_ref, peer, src_sem, dst_sem):
        return pltpu.make_async_remote_copy(
            src_ref=src_ref.at[peer],
            dst_ref=dst_ref.at[me],
            send_sem=src_sem,
            recv_sem=dst_sem,
            device_id={"lat": peer},
            device_id_type=MESH,
        )

    def send(step, carry):
        spread = step * 37 % lat_total
        peer = (line + spread // row_size) % columns * row_size
        peer = peer + (spot + spread // 2 % chips) % chips * 2 + (core + spread % 2) % 2
        to_peer(coeff_ref, recv_ref, peer, send_sem, recv_sem).start()
        return carry

    lax.fori_loop(1, lat_total, send, 0)
    own = pltpu.make_async_copy(coeff_ref.at[me], recv_ref.at[me], local_sem)
    own.start()
    pick = jnp.where(iota((lat_total, lat_total), 0) == order_ref[...], 1.0, 0.0).astype(BF16)
    slot_mat = jnp.dot(meridional_ref[0], pick, preferred_element_type=F32).astype(BF16)
    slot_mat = lax.dot_general(
        pick, slot_mat, (((0,), (0,)), ((), ())), preferred_element_type=F32
    ).astype(BF16)
    block = balance_ref[0]
    none = jnp.zeros_like(block)
    lift = jnp.concatenate(
        [jnp.concatenate([block, none], axis=1), jnp.concatenate([none, block], axis=1)], axis=0
    )
    own.wait()
    rest = pl.ds(0, lat_total - 1)

    def settle(ref, sem):
        pltpu.make_async_copy(ref.at[rest], ref.at[rest], sem).wait()

    settle(recv_ref, recv_sem)
    wide_ref[...] = recv_ref[...].astype(F32)
    received = [wide_ref[:, sub, :].astype(BF16) for sub in range(per_peer)]
    product = jnp.dot(slot_mat, jnp.concatenate(received, axis=1), preferred_element_type=F32)
    scaled = []
    for sub in range(per_peer):
        wave = 4 * (me % groups * per_peer + sub) + me // groups
        scaled.append(product[:, sub * LANES : (sub + 1) * LANES] * amp_ref[0, wave])
    product_ref[...] = jnp.concatenate(scaled, axis=1)

    def piece_rows(piece):
        there = (line + columns // 2 - piece + columns) % columns
        return there, pl.ds(pl.multiple_of(there * row_size, row_size), row_size)

    def root_copy(piece, target):
        _, here = piece_rows(piece)
        return pltpu.make_async_remote_copy(
            src_ref=root_ref.at[here],
            dst_ref=root_ref.at[here],
            send_sem=root_send_sem,
            recv_sem=root_recv_sem.at[piece],
            device_id={"var": target},
            device_id_type=MESH,
        )

    half = columns // 2
    relayed = var_total == 4

    @pl.when(var == 0)
    def _():
        root_ref[...] = product_ref[...].astype(BF16)
        for step in range(columns):
            if relayed:
                root_copy(step, 1).start()
                root_copy(columns - 1 - step, 3).start()
            else:
                for target in range(1, var_total):
                    root_copy(step, target).start()

    def one_piece(step, carry):
        outside_in = jnp.where(step % 2 == 0, step // 2, columns - 1 - step // 2)
        piece = jnp.where(var == 1, step, jnp.where(var == 3, columns - 1 - step, outside_in))
        there, here = piece_rows(piece)

        @pl.when(var > 0)
        def _():
            pltpu.make_async_copy(
                root_ref.at[here], root_ref.at[here], root_recv_sem.at[piece]
            ).wait()
            if relayed:

                @pl.when(((var == 1) & (piece < half)) | ((var == 3) & (piece >= half)))
                def _():
                    root_copy(piece, 2).start()

        part = root_ref[here, :]
        stacked = jnp.concatenate(
            [part[:, sub * LANES : (sub + 1) * LANES] for sub in range(per_peer)], axis=0
        )
        lifted = nt_dot(stacked, lift)
        derived = jnp.where(var > 0, 1.0, 0.0)
        for sub in range(per_peer):
            blended = product_ref[here, pl.ds(sub * LANES, LANES)]
            addend = lifted[sub * row_size : (sub + 1) * row_size]
            wide_ref[here, sub, :] = blended + jnp.where(var > 0, addend, 0.0)
        mixed_ref[here] = wide_ref[here].astype(BF16)

        def send_back(offset, inner):
            peer = there * row_size + (me + offset) % row_size

            @pl.when(peer != me)
            def _():
                to_peer(mixed_ref, balanced_ref, peer, back_send_sem, back_recv_sem).start()

            return inner

        lax.fori_loop(0, row_size, send_back, 0)
        return carry

    lax.fori_loop(0, columns, one_piece, 0)
    own = pltpu.make_async_copy(mixed_ref.at[me], balanced_ref.at[me], local_sem)
    own.start()
    own.wait()
    table_copy.wait()
    settle(coeff_ref, send_sem)

    def sent_roots(pieces):
        span = pl.ds(0, pieces * row_size)
        pltpu.make_async_copy(root_ref.at[span], root_ref.at[span], root_send_sem).wait()

    @pl.when(var == 0)
    def _():
        for _ in range(2 if relayed else var_total - 1):
            sent_roots(columns)

    if relayed:

        @pl.when((var == 1) | (var == 3))
        def _():
            sent_roots(half)

    settle(mixed_ref, back_send_sem)
    settle(balanced_ref, back_recv_sem)


def body(control, row_order, row_length, vertical, amplitude, meridional, balance):
    lat_total = row_order.shape[0]
    levels, lons = control.shape[2:]
    waves = amplitude.shape[1]
    per_peer = waves // lat_total
    groups = lat_total // 4
    quarter = lons // 4
    blocks = quarter // LANES
    vmem = pl.BlockSpec(memory_space=pltpu.VMEM)
    smem = pl.BlockSpec(memory_space=pltpu.SMEM)
    anywhere = pl.BlockSpec(memory_space=pl.ANY)
    seeds = pltpu.VMEM((groups + 4 * SUBS, quarter), F32)
    packed = jax.ShapeDtypeStruct((lat_total, SUBS, LANES), BF16)
    table = jax.ShapeDtypeStruct((2 * blocks, lat_total * SUBS, LANES), BF16)
    table_vmem = pltpu.VMEM(table.shape, BF16)
    block = pltpu.VMEM(packed.shape, BF16)
    dma = pltpu.SemaphoreType.DMA
    level = pltpu.VMEM((levels, lons + LANES), F32)
    balanced, basis = pl.pallas_call(
        functools.partial(blend_kernel, per_peer),
        name="blend",
        out_shape=(packed, table),
        in_specs=[smem, smem, smem, vmem, vmem, vmem, vmem, vmem],
        out_specs=(vmem, anywhere),
        scratch_shapes=[
            seeds,
            seeds,
            table_vmem,
            pltpu.VMEM((levels, lons + LANES), BF16),
            block,
            block,
            pltpu.VMEM(packed.shape, F32),
            pltpu.VMEM((lat_total, per_peer * LANES), F32),
            pltpu.VMEM((lat_total, per_peer * LANES), BF16),
            block,
            pltpu.SemaphoreType.REGULAR,
            dma(()),
            dma(()),
            dma(()),
            dma(()),
            dma(()),
            dma((lat_total,)),
            dma(()),
            dma(()),
        ],
        compiler_params=pltpu.CompilerParams(collective_id=0, has_side_effects=True),
    )(
        row_order,
        row_length,
        amplitude,
        row_order.reshape(1, lat_total),
        control,
        vertical,
        meridional,
        balance,
    )
    return pl.pallas_call(
        functools.partial(synthesis_kernel, per_peer),
        name="synthesis",
        out_shape=jax.ShapeDtypeStruct(control.shape, BF16),
        in_specs=[smem, smem, vmem, anywhere],
        out_specs=vmem,
        scratch_shapes=[table_vmem, level, dma((4,))],
    )(row_order, row_length, balanced, basis)


def solution(mesh):
    return jax.shard_map(
        body,
        mesh=mesh,
        in_specs=(
            P("var", "lat", None, None),
            P(),
            P(),
            P("var", None, None),
            P("var", None),
            P("var", None, None),
            P("var", None, None),
        ),
        out_specs=P("var", "lat", None, None),
        check_vma=False,
    )
```

```python
import functools
import math

import jax
import jax.numpy as jnp
from jax import lax
from jax.experimental import pallas as pl
from jax.experimental.pallas import tpu as pltpu
from jax.sharding import PartitionSpec as P

LANES = 128
SUBS = 8
ROW = 16
F32 = jnp.float32
BF16 = jnp.bfloat16
MESH = pl.DeviceIdType.MESH


def iota(shape, dim):
    return lax.broadcasted_iota(jnp.int32, shape, dim)


def nt_dot(a, b):
    return lax.dot_general(a, b, (((1,), (1,)), ((), ())), preferred_element_type=F32)


def own_length(order_ref, length_ref):
    return length_ref[order_ref[lax.axis_index("lat")]]


def wave_seeds(period, cos_ref, sin_ref, groups, per_peer):
    shape = cos_ref.shape
    row = iota(shape, 0)
    local = row - groups
    fine = 4 * (local % SUBS) + local // SUBS
    wave = jnp.where(row < groups, 4 * per_peer * row, fine).astype(F32)
    phase = wave * iota(shape, 1).astype(F32)
    inverse = 1.0 / period
    phase = phase - jnp.floor(phase * inverse + 0.5) * period
    quadrant = jnp.floor(phase * (4.0 * inverse) + 0.5)
    angle = (4.0 * phase - quadrant * period) * inverse * (0.5 * math.pi)
    sq = angle * angle
    sine = angle * (1.0 + sq * (-1.0 / 6 + sq * (1.0 / 120 + sq * (-1.0 / 5040 + sq * (1.0 / 362880)))))
    cosine = 1.0 + sq * (-0.5 + sq * (1.0 / 24 + sq * (-1.0 / 720 + sq * (1.0 / 40320))))
    odd = jnp.abs(quadrant) == 1.0
    flip = jnp.abs(quadrant) == 2.0
    sign = jnp.where(flip, -1.0, jnp.where(odd, quadrant, 1.0))
    cos_ref[...] = jnp.where(odd, -sign * sine, sign * cosine)
    sin_ref[...] = jnp.where(odd, sign * cosine, sign * sine)


def fill_table(cos_ref, sin_ref, table_ref, groups):
    blocks = table_ref.shape[0] // 2
    rows = groups * SUBS

    def one(step, carry):
        rem, blk = step // blocks, step % blocks
        cols = pl.ds(pl.multiple_of(blk * LANES, LANES), LANES)
        fine = pl.ds(pl.multiple_of(groups + rem * SUBS, SUBS), SUBS)
        cos_f, sin_f = cos_ref[fine, cols], sin_ref[fine, cols]
        for group in range(0, groups, 2):
            cosine, sine = [], []
            for g in (group, group + 1):
                cos_c, sin_c = cos_ref[pl.ds(g, 1), cols], sin_ref[pl.ds(g, 1), cols]
                cosine.append(cos_c * cos_f - sin_c * sin_f)
                sine.append(sin_c * cos_f + cos_c * sin_f)
            dest = pl.ds(pl.multiple_of(rem * rows + group * SUBS, 2 * SUBS), 2 * SUBS)
            table_ref[blk, dest, :] = jnp.concatenate(cosine, axis=0).astype(BF16)
            table_ref[blk + blocks, dest, :] = jnp.concatenate(sine, axis=0).astype(BF16)
        return carry

    lax.fori_loop(0, 4 * blocks, one, 0)


def table_rows(table_ref, rem, rows, first, last):
    here = pl.ds(rem * rows, rows)
    return jnp.concatenate([table_ref[b, here, :] for b in range(first, last)], axis=1)


def row_wave(lat_total, per_peer):
    groups = lat_total // 4
    shape = (lat_total, SUBS, LANES)
    peer = iota(shape, 0)
    sub = iota(shape, 1)
    wave = 4 * (peer % groups * per_peer + sub) + peer // groups
    return wave, sub < per_peer


def analyse(length, per_peer, control_ref, vertical_ref, coeff_ref, table_ref, level_ref):
    lat_total = coeff_ref.shape[0]
    groups = lat_total // 4
    rows = groups * SUBS
    lons = control_ref.shape[-1]
    quarter = lons // 4
    blocks = quarter // LANES
    period = length.astype(F32)
    levels = jnp.dot(vertical_ref[0], control_ref[0, 0], preferred_element_type=F32)
    level_ref[:, pl.ds(0, lons)] = levels.astype(BF16)
    level_ref[:, pl.ds(lons, LANES)] = jnp.zeros((levels.shape[0], LANES), BF16)
    count = levels.shape[0]
    step = length // 4
    lane = iota((count, LANES), 1)
    columns = [level_ref[:, pl.ds(b * LANES, LANES)] for b in range(4 * blocks + 1)]

    def shifted(part):
        base = part * step
        start, shift = base // LANES, base % LANES
        held = columns
        bit = 1 << max(part * blocks, 1).bit_length() - 1
        while bit and part:
            moved = [held[c + bit] if c + bit < len(held) else held[c] for c in range(len(held))]
            set_here = start // bit % 2 == 1
            held = [jnp.where(set_here, m, h) for m, h in zip(moved, held)]
            held = held[: blocks + bit]
            bit //= 2
        pairs = [jnp.concatenate([held[b], held[b + 1]], axis=1) for b in range(blocks)]
        if part:
            turn = (2 * LANES, LANES)
            place = jnp.where(iota(turn, 0) == iota(turn, 1) + shift, 1.0, 0.0).astype(BF16)
            both = jnp.dot(jnp.concatenate(pairs, axis=0), place, preferred_element_type=F32)
            parts = [both[b * count : (b + 1) * count] for b in range(blocks)]
        else:
            parts = [held[b].astype(F32) for b in range(blocks)]
        return jnp.concatenate(
            [jnp.where(lane + b * LANES < step, parts[b], 0.0) for b in range(blocks)], axis=1
        )

    x0, x1, x2, x3 = (shifted(q) for q in range(4))
    y0 = ((x0 + x2) + (x1 + x3)).astype(BF16)
    y2 = ((x0 + x2) - (x1 + x3)).astype(BF16)
    a = (x0 - x2).astype(BF16)
    b = (x1 - x3).astype(BF16)
    zero = jnp.zeros_like(y0)
    weights = (
        ((y0, zero), (zero, y0)),
        ((a, -b), (b, a)),
        ((y2, zero), (zero, y2)),
        ((a, b), (-b, a)),
    )
    wave, held = row_wave(lat_total, per_peer)
    scale = jnp.where(wave == 0, 1.0, 2.0) / period
    scale = jnp.where(held & (wave <= (length - 1) // 2), scale, 0.0)
    for rem in range(4):
        upper, lower = weights[rem]
        mixed = jnp.concatenate(
            [jnp.concatenate(upper, axis=1), jnp.concatenate(lower, axis=1)], axis=0
        )
        part = nt_dot(table_rows(table_ref, rem, rows, 0, 2 * blocks), mixed)
        part = part.reshape(groups, SUBS, LANES) * scale[rem * groups : (rem + 1) * groups]
        coeff_ref[pl.ds(rem * groups, groups)] = part.astype(BF16)


def synthesis_kernel(
    per_peer,
    order_hbm,
    length_hbm,
    balanced_hbm,
    table_hbm,
    out_hbm,
    order_ref,
    length_ref,
    balanced_ref,
    out_ref,
    table_ref,
    wide_ref,
    sems,
):
    lat_total = balanced_ref.shape[0]
    arriving = [
        pltpu.make_async_copy(source, target, sems.at[4 + index])
        for index, (source, target) in enumerate(
            ((order_hbm, order_ref), (length_hbm, length_ref), (balanced_hbm, balanced_ref))
        )
    ]
    for copy in arriving:
        copy.start()
    groups = lat_total // 4
    rows = groups * SUBS
    count, lons = out_ref.shape[-2], out_ref.shape[-1]
    quarter = lons // 4
    blocks = quarter // LANES
    loads = []
    for rem in range(4):
        here = pl.ds(rem * rows, rows)
        loads.append(
            pltpu.make_async_copy(table_hbm.at[:, here], table_ref.at[:, here], sems.at[rem])
        )
        loads[-1].start()
    wide_ref[...] = jnp.zeros_like(wide_ref)
    arriving[0].wait()
    arriving[1].wait()
    length = own_length(order_ref, length_ref)
    arriving[2].wait()
    wave, held = row_wave(lat_total, per_peer)
    spectra = jnp.where(
        held & (wave <= (length - 1) // 2), balanced_ref[...].astype(F32), 0.0
    )
    turned = spectra.reshape(lat_total * SUBS, LANES).T.astype(BF16)

    def parts(rem):
        both = turned[:, rem * rows : (rem + 1) * rows]
        return both[:count], both[count:]

    def against(rem, on_cos, on_sin):
        loads[rem].wait()
        return jnp.dot(
            on_cos, table_rows(table_ref, rem, rows, 0, blocks), preferred_element_type=F32
        ) + jnp.dot(
            on_sin, table_rows(table_ref, rem, rows, blocks, 2 * blocks), preferred_element_type=F32
        )

    c0, s0 = parts(0)
    c1, s1 = parts(1)
    c2, s2 = parts(2)
    c3, s3 = parts(3)
    e0 = against(0, c0, s0)
    e2 = against(2, c2, s2)
    ab = against(
        1, jnp.concatenate([c1, s1], axis=0), jnp.concatenate([s1, -c1], axis=0)
    ) + against(3, jnp.concatenate([c3, -s3], axis=0), jnp.concatenate([s3, c3], axis=0))
    a, b = ab[:count], ab[count:]
    step = length // 4
    lane = iota((count, LANES), 1)
    for part, piece in enumerate(((e0 + e2) + a, (e0 - e2) + b, (e0 + e2) - a, (e0 - e2) - b)):
        base = part * step
        start = base // LANES
        shift = base % LANES
        before = jnp.zeros((count, LANES), F32)
        for blk in range(blocks + 1):
            if blk < blocks:
                own = piece[:, blk * LANES : (blk + 1) * LANES]
                own = jnp.where(lane + blk * LANES < step, own, 0.0)
                rolled = pltpu.roll(own, shift, 1)
            else:
                rolled = jnp.zeros((count, LANES), F32)
            here = pl.ds(pl.multiple_of((start + blk) * LANES, LANES), LANES)
            wide_ref[:, here] += jnp.where(lane >= shift, rolled, before)
            before = rolled
    leaving = []
    for part in range(4):
        here = pl.ds(part * quarter, quarter)
        out_ref[:, here] = wide_ref[:, here].astype(BF16)
        leaving.append(
            pltpu.make_async_copy(out_ref.at[:, here], out_hbm.at[0, 0, :, here], sems.at[7 + part])
        )
        leaving[-1].start()
    for copy in leaving:
        copy.wait()


def blend_kernel(
    per_peer,
    order_hbm,
    length_hbm,
    amp_hbm,
    order_row_hbm,
    control_hbm,
    vertical_hbm,
    meridional_hbm,
    balance_hbm,
    balanced_ref,
    table_hbm,
    order_smem,
    length_ref,
    amp_ref,
    order_ref,
    control_ref,
    vertical_ref,
    meridional_ref,
    balance_ref,
    input_sems,
    cos_ref,
    sin_ref,
    table_ref,
    level_ref,
    coeff_ref,
    recv_ref,
    wide_ref,
    product_ref,
    root_ref,
    mixed_ref,
    line_sem,
    table_sem,
    local_sem,
    send_sem,
    recv_sem,
    root_send_sem,
    root_recv_sem,
    back_send_sem,
    back_recv_sem,
):
    lat_total = balanced_ref.shape[0]
    groups = lat_total // 4
    me = lax.axis_index("lat")
    var = lax.axis_index("var")
    var_total = lax.axis_size("var")
    row_size = ROW if lat_total % ROW == 0 else 2
    columns = lat_total // row_size
    chips = row_size // 2
    core, spot, line = me % 2, me // 2 % chips, me // row_size
    barrier = pltpu.get_barrier_semaphore()
    arriving = []
    for index, (source, target) in enumerate(
        (
            (order_hbm, order_smem),
            (length_hbm, length_ref),
            (vertical_hbm, vertical_ref),
            (control_hbm, control_ref),
            (amp_hbm, amp_ref),
            (order_row_hbm, order_ref),
            (meridional_hbm, meridional_ref),
            (balance_hbm, balance_ref),
        )
    ):
        arriving.append(pltpu.make_async_copy(source, target, input_sems.at[index]))

    def greet(sem, **where):
        pl.semaphore_signal(sem, 1, device_id=where, device_id_type=MESH)

    def greet_column(sem):
        for step in range(1, columns):
            greet(sem, lat=(line + step) % columns * row_size + me % row_size)

    arriving[0].start()
    arriving[1].start()
    for step in range(1, row_size):
        greet(barrier, lat=line * row_size + (me + step) % row_size)
    greet_column(barrier)
    for step in range(1, var_total):
        greet(barrier, var=(var + step) % var_total)
    for copy in arriving[2:]:
        copy.start()

    arriving[0].wait()
    arriving[1].wait()
    length = own_length(order_smem, length_ref)
    wave_seeds(length.astype(F32), cos_ref, sin_ref, groups, per_peer)
    fill_table(cos_ref, sin_ref, table_ref, groups)
    table_copy = pltpu.make_async_copy(table_ref, table_hbm, table_sem)
    table_copy.start()
    pl.semaphore_wait(barrier, row_size - 1 + columns - 1 + var_total - 1)
    greet_column(line_sem)
    arriving[2].wait()
    arriving[3].wait()
    analyse(length, per_peer, control_ref, vertical_ref, coeff_ref, table_ref, level_ref)
    pl.semaphore_wait(line_sem, columns - 1)

    def to_peer(src_ref, dst_ref, peer, src_sem, dst_sem):
        return pltpu.make_async_remote_copy(
            src_ref=src_ref.at[peer],
            dst_ref=dst_ref.at[me],
            send_sem=src_sem,
            recv_sem=dst_sem,
            device_id={"lat": peer},
            device_id_type=MESH,
        )

    def to_line(there, src_ref, dst_ref, src_sem, dst_sem):
        def one(offset, carry):
            peer = there * row_size + (me + offset) % row_size

            @pl.when(peer != me)
            def _():
                to_peer(src_ref, dst_ref, peer, src_sem, dst_sem).start()

            return carry

        lax.fori_loop(0, row_size, one, 0)

    def send(step, carry):
        to_line((line + columns // 2 + step) % columns, coeff_ref, recv_ref, send_sem, recv_sem)
        to_line((line + columns // 2 - step) % columns, coeff_ref, recv_ref, send_sem, recv_sem)
        return carry

    to_line((line + columns // 2) % columns, coeff_ref, recv_ref, send_sem, recv_sem)
    lax.fori_loop(1, columns // 2, send, 0)
    to_line(line, coeff_ref, recv_ref, send_sem, recv_sem)
    own = pltpu.make_async_copy(coeff_ref.at[me], recv_ref.at[me], local_sem)
    own.start()
    for copy in arriving[4:]:
        copy.wait()
    pick = jnp.where(iota((lat_total, lat_total), 0) == order_ref[...], 1.0, 0.0).astype(BF16)
    slot_mat = jnp.dot(meridional_ref[0], pick, preferred_element_type=F32).astype(BF16)
    slot_mat = lax.dot_general(
        pick, slot_mat, (((0,), (0,)), ((), ())), preferred_element_type=F32
    ).astype(BF16)
    block = balance_ref[0]
    none = jnp.zeros_like(block)
    lift = jnp.concatenate(
        [jnp.concatenate([block, none], axis=1), jnp.concatenate([none, block], axis=1)], axis=0
    )
    own.wait()
    rest = pl.ds(0, lat_total - 1)

    def settle(ref, sem):
        pltpu.make_async_copy(ref.at[rest], ref.at[rest], sem).wait()

    settle(recv_ref, recv_sem)
    wide_ref[...] = recv_ref[...].astype(F32)
    received = [wide_ref[:, sub, :].astype(BF16) for sub in range(per_peer)]
    product = jnp.dot(slot_mat, jnp.concatenate(received, axis=1), preferred_element_type=F32)
    scaled = []
    for sub in range(per_peer):
        wave = 4 * (me % groups * per_peer + sub) + me // groups
        scaled.append(product[:, sub * LANES : (sub + 1) * LANES] * amp_ref[0, wave])
    product_ref[...] = jnp.concatenate(scaled, axis=1)

    def piece_rows(piece):
        there = (line + columns // 2 - piece + columns) % columns
        return there, pl.ds(pl.multiple_of(there * row_size, row_size), row_size)

    def root_copy(piece, target):
        _, here = piece_rows(piece)
        return pltpu.make_async_remote_copy(
            src_ref=root_ref.at[here],
            dst_ref=root_ref.at[here],
            send_sem=root_send_sem,
            recv_sem=root_recv_sem.at[piece],
            device_id={"var": target},
            device_id_type=MESH,
        )

    half = columns // 2
    relayed = var_total == 4

    @pl.when(var == 0)
    def _():
        root_ref[...] = product_ref[...].astype(BF16)
        for step in range(columns):
            if relayed:
                root_copy(step, 1).start()
                root_copy(columns - 1 - step, 3).start()
            else:
                for target in range(1, var_total):
                    root_copy(step, target).start()

    def one_piece(step, carry):
        outside_in = jnp.where(step % 2 == 0, step // 2, columns - 1 - step // 2)
        piece = jnp.where(var == 1, step, jnp.where(var == 3, columns - 1 - step, outside_in))
        there, here = piece_rows(piece)

        @pl.when(var > 0)
        def _():
            pltpu.make_async_copy(
                root_ref.at[here], root_ref.at[here], root_recv_sem.at[piece]
            ).wait()
            if relayed:

                @pl.when(((var == 1) & (piece < half)) | ((var == 3) & (piece >= half)))
                def _():
                    root_copy(piece, 2).start()

        part = root_ref[here, :]
        stacked = jnp.concatenate(
            [part[:, sub * LANES : (sub + 1) * LANES] for sub in range(per_peer)], axis=0
        )
        lifted = nt_dot(stacked, lift)
        for sub in range(per_peer):
            blended = product_ref[here, pl.ds(sub * LANES, LANES)]
            addend = lifted[sub * row_size : (sub + 1) * row_size]
            wide_ref[here, sub, :] = blended + jnp.where(var > 0, addend, 0.0)
        mixed_ref[here] = wide_ref[here].astype(BF16)

        to_line(there, mixed_ref, balanced_ref, back_send_sem, back_recv_sem)
        return carry

    lax.fori_loop(0, columns, one_piece, 0)
    own = pltpu.make_async_copy(mixed_ref.at[me], balanced_ref.at[me], local_sem)
    own.start()
    own.wait()
    table_copy.wait()
    settle(coeff_ref, send_sem)

    def sent_roots(pieces):
        span = pl.ds(0, pieces * row_size)
        pltpu.make_async_copy(root_ref.at[span], root_ref.at[span], root_send_sem).wait()

    @pl.when(var == 0)
    def _():
        for _ in range(2 if relayed else var_total - 1):
            sent_roots(columns)

    if relayed:

        @pl.when((var == 1) | (var == 3))
        def _():
            sent_roots(half)

    settle(mixed_ref, back_send_sem)
    settle(balanced_ref, back_recv_sem)


def body(control, row_order, row_length, vertical, amplitude, meridional, balance):
    lat_total = row_order.shape[0]
    levels, lons = control.shape[2:]
    waves = amplitude.shape[1]
    per_peer = waves // lat_total
    groups = lat_total // 4
    quarter = lons // 4
    blocks = quarter // LANES
    vmem = pl.BlockSpec(memory_space=pltpu.VMEM)
    anywhere = pl.BlockSpec(memory_space=pl.ANY)
    seeds = pltpu.VMEM((groups + 4 * SUBS, quarter), F32)
    packed = jax.ShapeDtypeStruct((lat_total, SUBS, LANES), BF16)
    table = jax.ShapeDtypeStruct((2 * blocks, lat_total * SUBS, LANES), BF16)
    table_vmem = pltpu.VMEM(table.shape, BF16)
    block = pltpu.VMEM(packed.shape, BF16)
    dma = pltpu.SemaphoreType.DMA
    inputs = (
        pltpu.SMEM(row_order.shape, row_order.dtype),
        pltpu.SMEM(row_length.shape, row_length.dtype),
        pltpu.SMEM(amplitude.shape, F32),
        pltpu.VMEM((1, lat_total), row_order.dtype),
        pltpu.VMEM(control.shape, BF16),
        pltpu.VMEM(vertical.shape, BF16),
        pltpu.VMEM(meridional.shape, BF16),
        pltpu.VMEM(balance.shape, BF16),
    )
    balanced, basis = pl.pallas_call(
        functools.partial(blend_kernel, per_peer),
        name="blend",
        out_shape=(packed, table),
        in_specs=[anywhere] * 8,
        out_specs=(vmem, anywhere),
        scratch_shapes=[
            *inputs,
            dma((8,)),
            seeds,
            seeds,
            table_vmem,
            pltpu.VMEM((levels, lons + LANES), BF16),
            block,
            block,
            pltpu.VMEM(packed.shape, F32),
            pltpu.VMEM((lat_total, per_peer * LANES), F32),
            pltpu.VMEM((lat_total, per_peer * LANES), BF16),
            block,
            pltpu.SemaphoreType.REGULAR,
            dma(()),
            dma(()),
            dma(()),
            dma(()),
            dma(()),
            dma((lat_total,)),
            dma(()),
            dma(()),
        ],
        compiler_params=pltpu.CompilerParams(collective_id=0, has_side_effects=True),
    )(
        row_order,
        row_length,
        amplitude,
        row_order.reshape(1, lat_total),
        control,
        vertical,
        meridional,
        balance,
    )
    return pl.pallas_call(
        functools.partial(synthesis_kernel, per_peer),
        name="synthesis",
        out_shape=jax.ShapeDtypeStruct(control.shape, BF16),
        in_specs=[anywhere] * 4,
        out_specs=anywhere,
        scratch_shapes=[
            inputs[0],
            inputs[1],
            block,
            pltpu.VMEM((levels, lons), BF16),
            table_vmem,
            pltpu.VMEM((levels, lons + LANES), F32),
            dma((11,)),
        ],
    )(row_order, row_length, balanced, basis)


def solution(mesh):
    return jax.shard_map(
        body,
        mesh=mesh,
        in_specs=(
            P("var", "lat", None, None),
            P(),
            P(),
            P("var", None, None),
            P("var", None),
            P("var", None, None),
            P("var", None, None),
        ),
        out_specs=P("var", "lat", None, None),
        check_vma=False,
    )
```

```python
import functools
import math

import jax
import jax.numpy as jnp
from jax import lax
from jax.experimental import pallas as pl
from jax.experimental.pallas import tpu as pltpu
from jax.sharding import PartitionSpec as P

LANES = 128
SUBS = 8
ROW = 16
F32 = jnp.float32
BF16 = jnp.bfloat16
MESH = pl.DeviceIdType.MESH


def iota(shape, dim):
    return lax.broadcasted_iota(jnp.int32, shape, dim)


def nt_dot(a, b):
    return lax.dot_general(a, b, (((1,), (1,)), ((), ())), preferred_element_type=F32)


def own_length(order_ref, length_ref):
    return length_ref[order_ref[lax.axis_index("lat")]]


def wave_seeds(period, cos_ref, sin_ref, groups, per_peer):
    shape = cos_ref.shape
    row = iota(shape, 0)
    local = row - groups
    fine = 4 * (local % SUBS) + local // SUBS
    wave = jnp.where(row < groups, 4 * per_peer * row, fine).astype(F32)
    phase = wave * iota(shape, 1).astype(F32)
    inverse = 1.0 / period
    phase = phase - jnp.floor(phase * inverse + 0.5) * period
    quadrant = jnp.floor(phase * (4.0 * inverse) + 0.5)
    angle = (4.0 * phase - quadrant * period) * inverse * (0.5 * math.pi)
    sq = angle * angle
    sine = angle * (1.0 + sq * (-1.0 / 6 + sq * (1.0 / 120 + sq * (-1.0 / 5040 + sq * (1.0 / 362880)))))
    cosine = 1.0 + sq * (-0.5 + sq * (1.0 / 24 + sq * (-1.0 / 720 + sq * (1.0 / 40320))))
    odd = jnp.abs(quadrant) == 1.0
    flip = jnp.abs(quadrant) == 2.0
    sign = jnp.where(flip, -1.0, jnp.where(odd, quadrant, 1.0))
    cos_ref[...] = jnp.where(odd, -sign * sine, sign * cosine)
    sin_ref[...] = jnp.where(odd, sign * cosine, sign * sine)


def fill_table(cos_ref, sin_ref, table_ref, groups):
    blocks = table_ref.shape[0] // 2
    rows = groups * SUBS

    def one(step, carry):
        rem, blk = step // blocks, step % blocks
        cols = pl.ds(pl.multiple_of(blk * LANES, LANES), LANES)
        fine = pl.ds(pl.multiple_of(groups + rem * SUBS, SUBS), SUBS)
        cos_f, sin_f = cos_ref[fine, cols], sin_ref[fine, cols]
        for group in range(0, groups, 2):
            cosine, sine = [], []
            for g in (group, group + 1):
                cos_c, sin_c = cos_ref[pl.ds(g, 1), cols], sin_ref[pl.ds(g, 1), cols]
                cosine.append(cos_c * cos_f - sin_c * sin_f)
                sine.append(sin_c * cos_f + cos_c * sin_f)
            dest = pl.ds(pl.multiple_of(rem * rows + group * SUBS, 2 * SUBS), 2 * SUBS)
            table_ref[blk, dest, :] = jnp.concatenate(cosine, axis=0).astype(BF16)
            table_ref[blk + blocks, dest, :] = jnp.concatenate(sine, axis=0).astype(BF16)
        return carry

    lax.fori_loop(0, 4 * blocks, one, 0)


def table_rows(table_ref, rem, rows, first, last):
    here = pl.ds(rem * rows, rows)
    return jnp.concatenate([table_ref[b, here, :] for b in range(first, last)], axis=1)


def row_wave(lat_total, per_peer):
    groups = lat_total // 4
    shape = (lat_total, SUBS, LANES)
    peer = iota(shape, 0)
    sub = iota(shape, 1)
    wave = 4 * (peer % groups * per_peer + sub) + peer // groups
    return wave, sub < per_peer


def analyse(length, per_peer, control_ref, vertical_ref, coeff_ref, table_ref, level_ref):
    lat_total = coeff_ref.shape[0]
    groups = lat_total // 4
    rows = groups * SUBS
    lons = control_ref.shape[-1]
    quarter = lons // 4
    blocks = quarter // LANES
    period = length.astype(F32)
    levels = jnp.dot(vertical_ref[0], control_ref[0, 0], preferred_element_type=F32)
    level_ref[:, pl.ds(0, lons)] = levels.astype(BF16)
    level_ref[:, pl.ds(lons, LANES)] = jnp.zeros((levels.shape[0], LANES), BF16)
    count = levels.shape[0]
    step = length // 4
    lane = iota((count, LANES), 1)
    columns = [level_ref[:, pl.ds(b * LANES, LANES)] for b in range(4 * blocks + 1)]

    def shifted(part):
        base = part * step
        start, shift = base // LANES, base % LANES
        held = columns
        bit = 1 << max(part * blocks, 1).bit_length() - 1
        while bit and part:
            moved = [held[c + bit] if c + bit < len(held) else held[c] for c in range(len(held))]
            set_here = start // bit % 2 == 1
            held = [jnp.where(set_here, m, h) for m, h in zip(moved, held)]
            held = held[: blocks + bit]
            bit //= 2
        pairs = [jnp.concatenate([held[b], held[b + 1]], axis=1) for b in range(blocks)]
        if part:
            turn = (2 * LANES, LANES)
            place = jnp.where(iota(turn, 0) == iota(turn, 1) + shift, 1.0, 0.0).astype(BF16)
            both = jnp.dot(jnp.concatenate(pairs, axis=0), place, preferred_element_type=F32)
            parts = [both[b * count : (b + 1) * count] for b in range(blocks)]
        else:
            parts = [held[b].astype(F32) for b in range(blocks)]
        return jnp.concatenate(
            [jnp.where(lane + b * LANES < step, parts[b], 0.0) for b in range(blocks)], axis=1
        )

    x0, x1, x2, x3 = (shifted(q) for q in range(4))
    y0 = ((x0 + x2) + (x1 + x3)).astype(BF16)
    y2 = ((x0 + x2) - (x1 + x3)).astype(BF16)
    a = (x0 - x2).astype(BF16)
    b = (x1 - x3).astype(BF16)
    zero = jnp.zeros_like(y0)
    weights = (
        ((y0, zero), (zero, y0)),
        ((a, -b), (b, a)),
        ((y2, zero), (zero, y2)),
        ((a, b), (-b, a)),
    )
    wave, held = row_wave(lat_total, per_peer)
    scale = jnp.where(wave == 0, 1.0, 2.0) / period
    scale = jnp.where(held & (wave <= (length - 1) // 2), scale, 0.0)
    for rem in range(4):
        upper, lower = weights[rem]
        mixed = jnp.concatenate(
            [jnp.concatenate(upper, axis=1), jnp.concatenate(lower, axis=1)], axis=0
        )
        part = nt_dot(table_rows(table_ref, rem, rows, 0, 2 * blocks), mixed)
        part = part.reshape(groups, SUBS, LANES) * scale[rem * groups : (rem + 1) * groups]
        coeff_ref[pl.ds(rem * groups, groups)] = part.astype(BF16)


def synthesis_kernel(
    per_peer,
    order_hbm,
    length_hbm,
    balanced_hbm,
    table_hbm,
    out_hbm,
    order_ref,
    length_ref,
    balanced_ref,
    out_ref,
    table_ref,
    wide_ref,
    sems,
):
    lat_total = balanced_ref.shape[0]
    arriving = [
        pltpu.make_async_copy(source, target, sems.at[4 + index])
        for index, (source, target) in enumerate(
            ((order_hbm, order_ref), (length_hbm, length_ref), (balanced_hbm, balanced_ref))
        )
    ]
    for copy in arriving:
        copy.start()
    groups = lat_total // 4
    rows = groups * SUBS
    count, lons = out_ref.shape[-2], out_ref.shape[-1]
    quarter = lons // 4
    blocks = quarter // LANES
    loads = []
    for rem in range(4):
        here = pl.ds(rem * rows, rows)
        loads.append(
            pltpu.make_async_copy(table_hbm.at[:, here], table_ref.at[:, here], sems.at[rem])
        )
        loads[-1].start()
    wide_ref[...] = jnp.zeros_like(wide_ref)
    arriving[0].wait()
    arriving[1].wait()
    length = own_length(order_ref, length_ref)
    arriving[2].wait()
    wave, held = row_wave(lat_total, per_peer)
    spectra = jnp.where(
        held & (wave <= (length - 1) // 2), balanced_ref[...].astype(F32), 0.0
    )
    turned = spectra.reshape(lat_total * SUBS, LANES).T.astype(BF16)

    def parts(rem):
        both = turned[:, rem * rows : (rem + 1) * rows]
        return both[:count], both[count:]

    def against(rem, on_cos, on_sin):
        loads[rem].wait()
        return jnp.dot(
            on_cos, table_rows(table_ref, rem, rows, 0, blocks), preferred_element_type=F32
        ) + jnp.dot(
            on_sin, table_rows(table_ref, rem, rows, blocks, 2 * blocks), preferred_element_type=F32
        )

    c0, s0 = parts(0)
    c1, s1 = parts(1)
    c2, s2 = parts(2)
    c3, s3 = parts(3)
    e0 = against(0, c0, s0)
    e2 = against(2, c2, s2)
    ab = against(
        1, jnp.concatenate([c1, s1], axis=0), jnp.concatenate([s1, -c1], axis=0)
    ) + against(3, jnp.concatenate([c3, -s3], axis=0), jnp.concatenate([s3, c3], axis=0))
    a, b = ab[:count], ab[count:]
    step = length // 4
    lane = iota((count, LANES), 1)
    for part, piece in enumerate(((e0 + e2) + a, (e0 - e2) + b, (e0 + e2) - a, (e0 - e2) - b)):
        base = part * step
        start = base // LANES
        shift = base % LANES
        before = jnp.zeros((count, LANES), F32)
        for blk in range(blocks + 1):
            if blk < blocks:
                own = piece[:, blk * LANES : (blk + 1) * LANES]
                own = jnp.where(lane + blk * LANES < step, own, 0.0)
                rolled = pltpu.roll(own, shift, 1)
            else:
                rolled = jnp.zeros((count, LANES), F32)
            here = pl.ds(pl.multiple_of((start + blk) * LANES, LANES), LANES)
            wide_ref[:, here] += jnp.where(lane >= shift, rolled, before)
            before = rolled
    leaving = []
    for part in range(4):
        here = pl.ds(part * quarter, quarter)
        out_ref[:, here] = wide_ref[:, here].astype(BF16)
        leaving.append(
            pltpu.make_async_copy(out_ref.at[:, here], out_hbm.at[0, 0, :, here], sems.at[7 + part])
        )
        leaving[-1].start()
    for copy in leaving:
        copy.wait()


def blend_kernel(
    per_peer,
    order_hbm,
    length_hbm,
    amp_hbm,
    order_row_hbm,
    control_hbm,
    vertical_hbm,
    meridional_hbm,
    balance_hbm,
    balanced_hbm,
    table_hbm,
    order_smem,
    length_ref,
    amp_ref,
    order_ref,
    control_ref,
    vertical_ref,
    meridional_ref,
    balance_ref,
    input_sems,
    cos_ref,
    sin_ref,
    table_ref,
    level_ref,
    coeff_ref,
    recv_ref,
    wide_ref,
    product_ref,
    root_ref,
    mixed_ref,
    line_sem,
    table_sem,
    local_sem,
    send_sem,
    recv_sem,
    root_send_sem,
    root_recv_sem,
    back_send_sem,
    back_recv_sem,
):
    lat_total = balanced_hbm.shape[0]
    groups = lat_total // 4
    me = lax.axis_index("lat")
    var = lax.axis_index("var")
    var_total = lax.axis_size("var")
    row_size = ROW if lat_total % ROW == 0 else 2
    columns = lat_total // row_size
    chips = row_size // 2
    core, spot, line = me % 2, me // 2 % chips, me // row_size
    barrier = pltpu.get_barrier_semaphore()
    arriving = []
    for index, (source, target) in enumerate(
        (
            (order_hbm, order_smem),
            (length_hbm, length_ref),
            (vertical_hbm, vertical_ref),
            (control_hbm, control_ref),
            (amp_hbm, amp_ref),
            (order_row_hbm, order_ref),
            (meridional_hbm, meridional_ref),
            (balance_hbm, balance_ref),
        )
    ):
        arriving.append(pltpu.make_async_copy(source, target, input_sems.at[index]))

    def greet(sem, **where):
        pl.semaphore_signal(sem, 1, device_id=where, device_id_type=MESH)

    def greet_column(sem_of):
        for step in range(1, columns):
            greet(sem_of(step), lat=(line + step) % columns * row_size + me % row_size)

    arriving[0].start()
    arriving[1].start()
    for step in range(1, row_size):
        greet(barrier, lat=line * row_size + (me + step) % row_size)
    greet_column(lambda step: barrier)
    for step in range(1, var_total):
        greet(barrier, var=(var + step) % var_total)
    for copy in arriving[2:]:
        copy.start()

    arriving[0].wait()
    arriving[1].wait()
    length = own_length(order_smem, length_ref)
    wave_seeds(length.astype(F32), cos_ref, sin_ref, groups, per_peer)
    fill_table(cos_ref, sin_ref, table_ref, groups)
    table_copy = pltpu.make_async_copy(table_ref, table_hbm, table_sem)
    table_copy.start()
    pl.semaphore_wait(barrier, row_size - 1 + columns - 1 + var_total - 1)
    greet_column(lambda step: line_sem.at[columns - step])
    arriving[2].wait()
    arriving[3].wait()
    analyse(length, per_peer, control_ref, vertical_ref, coeff_ref, table_ref, level_ref)

    def to_peer(src_ref, dst_ref, peer, src_sem, dst_sem):
        return pltpu.make_async_remote_copy(
            src_ref=src_ref.at[peer],
            dst_ref=dst_ref.at[me],
            send_sem=src_sem,
            recv_sem=dst_sem,
            device_id={"lat": peer},
            device_id_type=MESH,
        )

    def to_line(there, src_ref, dst_ref, src_sem, dst_sem, own=None):
        def one(offset, carry):
            peer = there * row_size + (me + offset) % row_size

            def start():
                to_peer(src_ref, dst_ref, peer, src_sem, dst_sem).start()

            if own is None:
                pl.when(peer != me)(start)
            else:
                start()
            return carry

        lax.fori_loop(1 if own else 0, row_size, one, 0, unroll=True)

    def first(distance):
        pl.semaphore_wait(line_sem.at[distance], 1)
        there = (line + distance) % columns
        to_line(there, coeff_ref, recv_ref, send_sem, recv_sem, own=False)

    def send(step, carry):
        first(columns // 2 + step)
        first(columns // 2 - step)
        return carry

    to_line(line, coeff_ref, recv_ref, send_sem, recv_sem, own=True)
    first(columns // 2)
    lax.fori_loop(1, columns // 2, send, 0)
    own = pltpu.make_async_copy(coeff_ref.at[me], recv_ref.at[me], local_sem)
    own.start()
    for copy in arriving[4:]:
        copy.wait()
    pick = jnp.where(iota((lat_total, lat_total), 0) == order_ref[...], 1.0, 0.0).astype(BF16)
    slot_mat = jnp.dot(meridional_ref[0], pick, preferred_element_type=F32).astype(BF16)
    slot_mat = lax.dot_general(
        pick, slot_mat, (((0,), (0,)), ((), ())), preferred_element_type=F32
    ).astype(BF16)
    block = balance_ref[0]
    none = jnp.zeros_like(block)
    lift = jnp.concatenate(
        [jnp.concatenate([block, none], axis=1), jnp.concatenate([none, block], axis=1)], axis=0
    )
    own.wait()
    rest = pl.ds(0, lat_total - 1)

    def settle(ref, sem):
        pltpu.make_async_copy(ref.at[rest], ref.at[rest], sem).wait()

    settle(recv_ref, recv_sem)
    wide_ref[...] = recv_ref[...].astype(F32)
    received = [wide_ref[:, sub, :].astype(BF16) for sub in range(per_peer)]
    product = jnp.dot(slot_mat, jnp.concatenate(received, axis=1), preferred_element_type=F32)
    scaled = []
    for sub in range(per_peer):
        wave = 4 * (me % groups * per_peer + sub) + me // groups
        scaled.append(product[:, sub * LANES : (sub + 1) * LANES] * amp_ref[0, wave])
    product_ref[...] = jnp.concatenate(scaled, axis=1)

    def piece_rows(piece):
        there = (line + columns // 2 + piece) % columns
        return there, pl.ds(pl.multiple_of(there * row_size, row_size), row_size)

    def root_copy(piece, target):
        _, here = piece_rows(piece)
        return pltpu.make_async_remote_copy(
            src_ref=root_ref.at[here],
            dst_ref=root_ref.at[here],
            send_sem=root_send_sem,
            recv_sem=root_recv_sem.at[piece],
            device_id={"var": target},
            device_id_type=MESH,
        )

    half = columns // 2
    relayed = var_total == 4

    @pl.when(var == 0)
    def _():
        root_ref[...] = product_ref[...].astype(BF16)
        for step in range(columns):
            if relayed:
                root_copy(step, 1).start()
                root_copy(columns - 1 - step, 3).start()
            else:
                for target in range(1, var_total):
                    root_copy(step, target).start()

    def await_root(piece):
        _, here = piece_rows(piece)
        pltpu.make_async_copy(root_ref.at[here], root_ref.at[here], root_recv_sem.at[piece]).wait()

    if relayed:
        @pl.when((var == 1) | (var == 3))
        def _():
            def relay(step, carry):
                piece = jnp.where(var == 1, step, columns - 1 - step)
                await_root(piece)
                root_copy(piece, 2).start()
                return carry

            lax.fori_loop(0, half, relay, 0)

    def one_piece(step, carry):
        outside_in = jnp.where(step % 2 == 0, step // 2, columns - 1 - step // 2)
        piece = jnp.where(var == 1, step, jnp.where(var == 3, columns - 1 - step, outside_in))
        there, here = piece_rows(piece)

        waiting = var > 0
        if relayed:
            passed_on = ((var == 1) & (piece < half)) | ((var == 3) & (piece >= half))
            waiting = waiting & jnp.logical_not(passed_on)

        @pl.when(waiting)
        def _():
            await_root(piece)

        part = root_ref[here, :]
        stacked = jnp.concatenate(
            [part[:, sub * LANES : (sub + 1) * LANES] for sub in range(per_peer)], axis=0
        )
        lifted = nt_dot(stacked, lift)
        for sub in range(per_peer):
            blended = product_ref[here, pl.ds(sub * LANES, LANES)]
            addend = lifted[sub * row_size : (sub + 1) * row_size]
            wide_ref[here, sub, :] = blended + jnp.where(var > 0, addend, 0.0)
        mixed_ref[here] = wide_ref[here].astype(BF16)

        to_line(there, mixed_ref, balanced_hbm, back_send_sem, back_recv_sem)
        return carry

    lax.fori_loop(0, columns, one_piece, 0)
    own = pltpu.make_async_copy(mixed_ref.at[me], balanced_hbm.at[me], local_sem)
    own.start()
    own.wait()
    table_copy.wait()
    settle(coeff_ref, send_sem)

    def sent_roots(pieces):
        span = pl.ds(0, pieces * row_size)
        pltpu.make_async_copy(root_ref.at[span], root_ref.at[span], root_send_sem).wait()

    @pl.when(var == 0)
    def _():
        for _ in range(2 if relayed else var_total - 1):
            sent_roots(columns)

    if relayed:

        @pl.when((var == 1) | (var == 3))
        def _():
            sent_roots(half)

    settle(mixed_ref, back_send_sem)
    settle(balanced_hbm, back_recv_sem)


def body(control, row_order, row_length, vertical, amplitude, meridional, balance):
    lat_total = row_order.shape[0]
    levels, lons = control.shape[2:]
    waves = amplitude.shape[1]
    per_peer = waves // lat_total
    groups = lat_total // 4
    quarter = lons // 4
    blocks = quarter // LANES
    anywhere = pl.BlockSpec(memory_space=pl.ANY)
    seeds = pltpu.VMEM((groups + 4 * SUBS, quarter), F32)
    packed = jax.ShapeDtypeStruct((lat_total, SUBS, LANES), BF16)
    table = jax.ShapeDtypeStruct((2 * blocks, lat_total * SUBS, LANES), BF16)
    table_vmem = pltpu.VMEM(table.shape, BF16)
    block = pltpu.VMEM(packed.shape, BF16)
    dma = pltpu.SemaphoreType.DMA
    inputs = (
        pltpu.SMEM(row_order.shape, row_order.dtype),
        pltpu.SMEM(row_length.shape, row_length.dtype),
        pltpu.SMEM(amplitude.shape, F32),
        pltpu.VMEM((1, lat_total), row_order.dtype),
        pltpu.VMEM(control.shape, BF16),
        pltpu.VMEM(vertical.shape, BF16),
        pltpu.VMEM(meridional.shape, BF16),
        pltpu.VMEM(balance.shape, BF16),
    )
    balanced, basis = pl.pallas_call(
        functools.partial(blend_kernel, per_peer),
        name="blend",
        out_shape=(packed, table),
        in_specs=[anywhere] * 8,
        out_specs=(anywhere, anywhere),
        scratch_shapes=[
            *inputs,
            dma((8,)),
            seeds,
            seeds,
            table_vmem,
            pltpu.VMEM((levels, lons + LANES), BF16),
            block,
            block,
            pltpu.VMEM(packed.shape, F32),
            pltpu.VMEM((lat_total, per_peer * LANES), F32),
            pltpu.VMEM((lat_total, per_peer * LANES), BF16),
            block,
            pltpu.SemaphoreType.REGULAR((lat_total,)),
            dma(()),
            dma(()),
            dma(()),
            dma(()),
            dma(()),
            dma((lat_total,)),
            dma(()),
            dma(()),
        ],
        compiler_params=pltpu.CompilerParams(collective_id=0, has_side_effects=True),
    )(
        row_order,
        row_length,
        amplitude,
        row_order.reshape(1, lat_total),
        control,
        vertical,
        meridional,
        balance,
    )
    return pl.pallas_call(
        functools.partial(synthesis_kernel, per_peer),
        name="synthesis",
        out_shape=jax.ShapeDtypeStruct(control.shape, BF16),
        in_specs=[anywhere] * 4,
        out_specs=anywhere,
        scratch_shapes=[
            inputs[0],
            inputs[1],
            block,
            pltpu.VMEM((levels, lons), BF16),
            table_vmem,
            pltpu.VMEM((levels, lons + LANES), F32),
            dma((11,)),
        ],
    )(row_order, row_length, balanced, basis)


def solution(mesh):
    return jax.shard_map(
        body,
        mesh=mesh,
        in_specs=(
            P("var", "lat", None, None),
            P(),
            P(),
            P("var", None, None),
            P("var", None),
            P("var", None, None),
            P("var", None, None),
        ),
        out_specs=P("var", "lat", None, None),
        check_vma=False,
    )
```

```python
import functools
import math

import jax
import jax.numpy as jnp
from jax import lax
from jax.experimental import pallas as pl
from jax.experimental.pallas import tpu as pltpu
from jax.sharding import PartitionSpec as P

LANES = 128
SUBS = 8
ROW = 16
F32 = jnp.float32
BF16 = jnp.bfloat16
MESH = pl.DeviceIdType.MESH


def iota(shape, dim):
    return lax.broadcasted_iota(jnp.int32, shape, dim)


def nt_dot(a, b):
    return lax.dot_general(a, b, (((1,), (1,)), ((), ())), preferred_element_type=F32)


def row_of(lat_total):
    return ROW if lat_total % ROW == 0 else 2


def own_length(order_ref, length_ref):
    return length_ref[order_ref[lax.axis_index("lat")]]


def wave_seeds(period, cos_ref, sin_ref, groups, per_peer):
    shape = cos_ref.shape
    row = iota(shape, 0)
    local = row - groups
    fine = 4 * (local % SUBS) + local // SUBS
    wave = jnp.where(row < groups, 4 * per_peer * row, fine).astype(F32)
    phase = wave * iota(shape, 1).astype(F32)
    inverse = 1.0 / period
    phase = phase - jnp.floor(phase * inverse + 0.5) * period
    quadrant = jnp.floor(phase * (4.0 * inverse) + 0.5)
    angle = (4.0 * phase - quadrant * period) * inverse * (0.5 * math.pi)
    sq = angle * angle
    sine = angle * (1.0 + sq * (-1.0 / 6 + sq * (1.0 / 120 + sq * (-1.0 / 5040 + sq * (1.0 / 362880)))))
    cosine = 1.0 + sq * (-0.5 + sq * (1.0 / 24 + sq * (-1.0 / 720 + sq * (1.0 / 40320))))
    odd = jnp.abs(quadrant) == 1.0
    flip = jnp.abs(quadrant) == 2.0
    sign = jnp.where(flip, -1.0, jnp.where(odd, quadrant, 1.0))
    cos_ref[...] = jnp.where(odd, -sign * sine, sign * cosine)
    sin_ref[...] = jnp.where(odd, sign * cosine, sign * sine)


def fill_table(cos_ref, sin_ref, table_ref, groups):
    blocks = table_ref.shape[0] // 2
    rows = groups * SUBS

    def one(step, carry):
        rem, blk = step // blocks, step % blocks
        cols = pl.ds(pl.multiple_of(blk * LANES, LANES), LANES)
        fine = pl.ds(pl.multiple_of(groups + rem * SUBS, SUBS), SUBS)
        cos_f, sin_f = cos_ref[fine, cols], sin_ref[fine, cols]
        for group in range(0, groups, 2):
            cosine, sine = [], []
            for g in (group, group + 1):
                cos_c, sin_c = cos_ref[pl.ds(g, 1), cols], sin_ref[pl.ds(g, 1), cols]
                cosine.append(cos_c * cos_f - sin_c * sin_f)
                sine.append(sin_c * cos_f + cos_c * sin_f)
            dest = pl.ds(pl.multiple_of(rem * rows + group * SUBS, 2 * SUBS), 2 * SUBS)
            table_ref[blk, dest, :] = jnp.concatenate(cosine, axis=0).astype(BF16)
            table_ref[blk + blocks, dest, :] = jnp.concatenate(sine, axis=0).astype(BF16)
        return carry

    lax.fori_loop(0, 4 * blocks, one, 0)


def table_rows(table_ref, rem, rows, first, last):
    here = pl.ds(rem * rows, rows)
    return jnp.concatenate([table_ref[b, here, :] for b in range(first, last)], axis=1)


def row_wave(lat_total, per_peer):
    groups = lat_total // 4
    shape = (lat_total, SUBS, LANES)
    peer = iota(shape, 0)
    sub = iota(shape, 1)
    wave = 4 * (peer % groups * per_peer + sub) + peer // groups
    return wave, sub < per_peer


def analyse(length, per_peer, control_ref, vertical_ref, coeff_ref, table_ref, level_ref):
    lat_total = coeff_ref.shape[0]
    groups = lat_total // 4
    rows = groups * SUBS
    lons = control_ref.shape[-1]
    quarter = lons // 4
    blocks = quarter // LANES
    period = length.astype(F32)
    levels = jnp.dot(vertical_ref[0], control_ref[0, 0], preferred_element_type=F32)
    level_ref[:, pl.ds(0, lons)] = levels.astype(BF16)
    level_ref[:, pl.ds(lons, LANES)] = jnp.zeros((levels.shape[0], LANES), BF16)
    count = levels.shape[0]
    step = length // 4
    lane = iota((count, LANES), 1)
    columns = [level_ref[:, pl.ds(b * LANES, LANES)] for b in range(4 * blocks + 1)]

    def shifted(part):
        base = part * step
        start, shift = base // LANES, base % LANES
        held = columns
        bit = 1 << max(part * blocks, 1).bit_length() - 1
        while bit and part:
            moved = [held[c + bit] if c + bit < len(held) else held[c] for c in range(len(held))]
            set_here = start // bit % 2 == 1
            held = [jnp.where(set_here, m, h) for m, h in zip(moved, held)]
            held = held[: blocks + bit]
            bit //= 2
        pairs = [jnp.concatenate([held[b], held[b + 1]], axis=1) for b in range(blocks)]
        if part:
            turn = (2 * LANES, LANES)
            place = jnp.where(iota(turn, 0) == iota(turn, 1) + shift, 1.0, 0.0).astype(BF16)
            both = jnp.dot(jnp.concatenate(pairs, axis=0), place, preferred_element_type=F32)
            parts = [both[b * count : (b + 1) * count] for b in range(blocks)]
        else:
            parts = [held[b].astype(F32) for b in range(blocks)]
        return jnp.concatenate(
            [jnp.where(lane + b * LANES < step, parts[b], 0.0) for b in range(blocks)], axis=1
        )

    x0, x1, x2, x3 = (shifted(q) for q in range(4))
    y0 = ((x0 + x2) + (x1 + x3)).astype(BF16)
    y2 = ((x0 + x2) - (x1 + x3)).astype(BF16)
    a = (x0 - x2).astype(BF16)
    b = (x1 - x3).astype(BF16)
    zero = jnp.zeros_like(y0)
    weights = (
        ((y0, zero), (zero, y0)),
        ((a, -b), (b, a)),
        ((y2, zero), (zero, y2)),
        ((a, b), (-b, a)),
    )
    wave, held = row_wave(lat_total, per_peer)
    scale = jnp.where(wave == 0, 1.0, 2.0) / period
    scale = jnp.where(held & (wave <= (length - 1) // 2), scale, 0.0)
    for rem in range(4):
        upper, lower = weights[rem]
        mixed = jnp.concatenate(
            [jnp.concatenate(upper, axis=1), jnp.concatenate(lower, axis=1)], axis=0
        )
        part = nt_dot(table_rows(table_ref, rem, rows, 0, 2 * blocks), mixed)
        part = part.reshape(groups, SUBS, LANES) * scale[rem * groups : (rem + 1) * groups]
        coeff_ref[pl.ds(rem * groups, groups)] = part.astype(BF16)


def synthesis_kernel(
    per_peer,
    order_hbm,
    length_hbm,
    balanced_hbm,
    table_hbm,
    out_hbm,
    order_ref,
    length_ref,
    balanced_ref,
    out_ref,
    table_ref,
    wide_ref,
    sems,
):
    lat_total = balanced_ref.shape[0]
    arriving = [
        pltpu.make_async_copy(source, target, sems.at[4 + index])
        for index, (source, target) in enumerate(
            ((order_hbm, order_ref), (length_hbm, length_ref), (balanced_hbm, balanced_ref))
        )
    ]
    for copy in arriving:
        copy.start()
    groups = lat_total // 4
    rows = groups * SUBS
    count, lons = out_ref.shape[-2], out_ref.shape[-1]
    quarter = lons // 4
    blocks = quarter // LANES
    loads = []
    for rem in range(4):
        here = pl.ds(rem * rows, rows)
        loads.append(
            pltpu.make_async_copy(table_hbm.at[:, here], table_ref.at[:, here], sems.at[rem])
        )
        loads[-1].start()
    wide_ref[...] = jnp.zeros_like(wide_ref)
    arriving[0].wait()
    arriving[1].wait()
    length = own_length(order_ref, length_ref)
    arriving[2].wait()
    wave, held = row_wave(lat_total, per_peer)
    spectra = jnp.where(
        held & (wave <= (length - 1) // 2), balanced_ref[...].astype(F32), 0.0
    )
    turned = spectra.reshape(lat_total * SUBS, LANES).T.astype(BF16)

    def parts(rem):
        both = turned[:, rem * rows : (rem + 1) * rows]
        return both[:count], both[count:]

    def against(rem, on_cos, on_sin):
        loads[rem].wait()
        return jnp.dot(
            on_cos, table_rows(table_ref, rem, rows, 0, blocks), preferred_element_type=F32
        ) + jnp.dot(
            on_sin, table_rows(table_ref, rem, rows, blocks, 2 * blocks), preferred_element_type=F32
        )

    c0, s0 = parts(0)
    c1, s1 = parts(1)
    c2, s2 = parts(2)
    c3, s3 = parts(3)
    e0 = against(0, c0, s0)
    e2 = against(2, c2, s2)
    ab = against(
        1, jnp.concatenate([c1, s1], axis=0), jnp.concatenate([s1, -c1], axis=0)
    ) + against(3, jnp.concatenate([c3, -s3], axis=0), jnp.concatenate([s3, c3], axis=0))
    a, b = ab[:count], ab[count:]
    step = length // 4
    lane = iota((count, LANES), 1)
    for part, piece in enumerate(((e0 + e2) + a, (e0 - e2) + b, (e0 + e2) - a, (e0 - e2) - b)):
        base = part * step
        start = base // LANES
        shift = base % LANES
        before = jnp.zeros((count, LANES), F32)
        for blk in range(blocks + 1):
            if blk < blocks:
                own = piece[:, blk * LANES : (blk + 1) * LANES]
                own = jnp.where(lane + blk * LANES < step, own, 0.0)
                rolled = pltpu.roll(own, shift, 1)
            else:
                rolled = jnp.zeros((count, LANES), F32)
            here = pl.ds(pl.multiple_of((start + blk) * LANES, LANES), LANES)
            wide_ref[:, here] += jnp.where(lane >= shift, rolled, before)
            before = rolled
    leaving = []
    for part in range(4):
        here = pl.ds(part * quarter, quarter)
        out_ref[:, here] = wide_ref[:, here].astype(BF16)
        leaving.append(
            pltpu.make_async_copy(out_ref.at[:, here], out_hbm.at[0, 0, :, here], sems.at[7 + part])
        )
        leaving[-1].start()
    for copy in leaving:
        copy.wait()


def blend_kernel(
    per_peer,
    order_hbm,
    length_hbm,
    amp_hbm,
    order_row_hbm,
    control_hbm,
    vertical_hbm,
    meridional_hbm,
    balance_hbm,
    balanced_hbm,
    table_hbm,
    order_smem,
    length_ref,
    amp_ref,
    order_ref,
    control_ref,
    vertical_ref,
    meridional_ref,
    balance_ref,
    input_sems,
    cos_ref,
    sin_ref,
    table_ref,
    level_ref,
    coeff_ref,
    recv_ref,
    wide_ref,
    product_ref,
    root_ref,
    mixed_ref,
    line_sem,
    table_sem,
    local_sem,
    send_sem,
    recv_sem,
    root_send_sem,
    root_recv_sem,
    back_send_sem,
    back_recv_sem,
):
    lat_total = balanced_hbm.shape[0]
    groups = lat_total // 4
    me = lax.axis_index("lat")
    var = lax.axis_index("var")
    var_total = lax.axis_size("var")
    row_size = row_of(lat_total)
    columns = lat_total // row_size
    chips = row_size // 2
    core, spot, line = me % 2, me // 2 % chips, me // row_size
    barrier = pltpu.get_barrier_semaphore()
    arriving = []
    for index, (source, target) in enumerate(
        (
            (order_hbm, order_smem),
            (length_hbm, length_ref),
            (vertical_hbm, vertical_ref),
            (control_hbm, control_ref),
            (amp_hbm, amp_ref),
            (order_row_hbm, order_ref),
            (meridional_hbm, meridional_ref),
            (balance_hbm, balance_ref),
        )
    ):
        arriving.append(pltpu.make_async_copy(source, target, input_sems.at[index]))

    def greet(sem, **where):
        pl.semaphore_signal(sem, 1, device_id=where, device_id_type=MESH)

    def greet_column(sem):
        for step in range(1, columns):
            greet(sem, lat=(line + step) % columns * row_size + me % row_size)

    arriving[0].start()
    arriving[1].start()
    for step in range(1, row_size):
        greet(barrier, lat=line * row_size + (me + step) % row_size)
    greet_column(barrier)
    for step in range(1, var_total):
        greet(barrier, var=(var + step) % var_total)
    for copy in arriving[2:]:
        copy.start()

    arriving[0].wait()
    arriving[1].wait()
    length = own_length(order_smem, length_ref)
    wave_seeds(length.astype(F32), cos_ref, sin_ref, groups, per_peer)
    fill_table(cos_ref, sin_ref, table_ref, groups)
    table_copy = pltpu.make_async_copy(table_ref, table_hbm, table_sem)
    table_copy.start()
    pl.semaphore_wait(barrier, row_size - 1 + columns - 1 + var_total - 1)
    greet_column(line_sem)
    arriving[2].wait()
    arriving[3].wait()
    analyse(length, per_peer, control_ref, vertical_ref, coeff_ref, table_ref, level_ref)
    pl.semaphore_wait(line_sem, columns - 1)

    def to_peer(src_ref, dst_ref, peer, src_sem, dst_sem):
        return pltpu.make_async_remote_copy(
            src_ref=src_ref.at[peer],
            dst_ref=dst_ref.at[me],
            send_sem=src_sem,
            recv_sem=dst_sem,
            device_id={"lat": peer},
            device_id_type=MESH,
        )

    def to_line(there, src_ref, dst_ref, src_sem, dst_sem, own=None):
        def one(offset, carry):
            peer = there * row_size + (me + offset) % row_size

            def start():
                to_peer(src_ref, dst_ref, peer, src_sem, dst_sem).start()

            if own is None:
                pl.when(peer != me)(start)
            else:
                start()
            return carry

        lax.fori_loop(1 if own else 0, row_size, one, 0, unroll=True)

    def first(there, own=False):
        to_line(there, coeff_ref, recv_ref, send_sem, recv_sem, own)

    def send(step, carry):
        first((line + columns // 2 + step) % columns)
        first((line + columns // 2 - step) % columns)
        return carry

    first((line + columns // 2) % columns)
    lax.fori_loop(1, columns // 2, send, 0)
    first(line, own=True)
    own = pltpu.make_async_copy(coeff_ref.at[me], recv_ref.at[me], local_sem)
    own.start()
    for copy in arriving[4:]:
        copy.wait()
    pick = jnp.where(iota((lat_total, lat_total), 0) == order_ref[...], 1.0, 0.0).astype(BF16)
    slot_mat = jnp.dot(meridional_ref[0], pick, preferred_element_type=F32).astype(BF16)
    slot_mat = lax.dot_general(
        pick, slot_mat, (((0,), (0,)), ((), ())), preferred_element_type=F32
    ).astype(BF16)
    block = balance_ref[0]
    none = jnp.zeros_like(block)
    lift = jnp.concatenate(
        [jnp.concatenate([block, none], axis=1), jnp.concatenate([none, block], axis=1)], axis=0
    )
    own.wait()
    rest = pl.ds(0, lat_total - 1)

    def settle(ref, sem):
        pltpu.make_async_copy(ref.at[rest], ref.at[rest], sem).wait()

    settle(recv_ref, recv_sem)
    wide_ref[...] = recv_ref[...].astype(F32)
    received = [wide_ref[:, sub, :].astype(BF16) for sub in range(per_peer)]
    product = jnp.dot(slot_mat, jnp.concatenate(received, axis=1), preferred_element_type=F32)
    scaled = []
    for sub in range(per_peer):
        wave = 4 * (me % groups * per_peer + sub) + me // groups
        scaled.append(product[:, sub * LANES : (sub + 1) * LANES] * amp_ref[0, wave])
    product_ref[...] = jnp.concatenate(scaled, axis=1)

    def piece_rows(piece):
        there = (line + columns // 2 + piece) % columns
        return there, pl.ds(pl.multiple_of(there * row_size, row_size), row_size)

    def root_copy(piece, target):
        _, here = piece_rows(piece)
        return pltpu.make_async_remote_copy(
            src_ref=root_ref.at[here],
            dst_ref=root_ref.at[here],
            send_sem=root_send_sem,
            recv_sem=root_recv_sem.at[piece],
            device_id={"var": target},
            device_id_type=MESH,
        )

    half = columns // 2
    relayed = var_total == 4

    @pl.when(var == 0)
    def _():
        root_ref[...] = product_ref[...].astype(BF16)
        for step in range(columns):
            if relayed:
                root_copy(step, 1).start()
                root_copy(columns - 1 - step, 3).start()
            else:
                for target in range(1, var_total):
                    root_copy(step, target).start()

    def await_root(piece):
        _, here = piece_rows(piece)
        pltpu.make_async_copy(root_ref.at[here], root_ref.at[here], root_recv_sem.at[piece]).wait()

    def relay(step):
        piece = jnp.where(var == 1, step, columns - 1 - step)
        await_root(piece)
        root_copy(piece, 2).start()

    between = (var == 1) | (var == 3)
    if relayed:
        pl.when(between)(lambda: relay(0))

    def one_piece(step, carry):
        outside_in = jnp.where(step % 2 == 0, step // 2, columns - 1 - step // 2)
        piece = jnp.where(var == 1, step, jnp.where(var == 3, columns - 1 - step, outside_in))
        there, here = piece_rows(piece)
        if relayed:
            pl.when(between & (step + 1 < half))(lambda: relay(step + 1))

        waiting = var > 0
        if relayed:
            passed_on = ((var == 1) & (piece < half)) | ((var == 3) & (piece >= half))
            waiting = waiting & jnp.logical_not(passed_on)

        @pl.when(waiting)
        def _():
            await_root(piece)

        part = root_ref[here, :]
        stacked = jnp.concatenate(
            [part[:, sub * LANES : (sub + 1) * LANES] for sub in range(per_peer)], axis=0
        )
        lifted = nt_dot(stacked, lift)
        for sub in range(per_peer):
            blended = product_ref[here, pl.ds(sub * LANES, LANES)]
            addend = lifted[sub * row_size : (sub + 1) * row_size]
            wide_ref[here, sub, :] = blended + jnp.where(var > 0, addend, 0.0)
        mixed_ref[here] = wide_ref[here].astype(BF16)

        to_line(there, mixed_ref, balanced_hbm, back_send_sem, back_recv_sem)
        return carry

    lax.fori_loop(0, columns, one_piece, 0)
    own = pltpu.make_async_copy(mixed_ref.at[me], balanced_hbm.at[me], local_sem)
    own.start()
    own.wait()
    table_copy.wait()
    settle(coeff_ref, send_sem)

    def sent_roots(pieces):
        span = pl.ds(0, pieces * row_size)
        pltpu.make_async_copy(root_ref.at[span], root_ref.at[span], root_send_sem).wait()

    @pl.when(var == 0)
    def _():
        for _ in range(2 if relayed else var_total - 1):
            sent_roots(columns)

    if relayed:

        @pl.when(between)
        def _():
            sent_roots(half)

    settle(mixed_ref, back_send_sem)
    settle(balanced_hbm, back_recv_sem)


def body(control, row_order, row_length, vertical, amplitude, meridional, balance):
    lat_total = row_order.shape[0]
    levels, lons = control.shape[2:]
    waves = amplitude.shape[1]
    per_peer = waves // lat_total
    groups = lat_total // 4
    quarter = lons // 4
    blocks = quarter // LANES
    columns = lat_total // row_of(lat_total)
    anywhere = pl.BlockSpec(memory_space=pl.ANY)
    seeds = pltpu.VMEM((groups + 4 * SUBS, quarter), F32)
    packed = jax.ShapeDtypeStruct((lat_total, SUBS, LANES), BF16)
    table = jax.ShapeDtypeStruct((2 * blocks, lat_total * SUBS, LANES), BF16)
    table_vmem = pltpu.VMEM(table.shape, BF16)
    block = pltpu.VMEM(packed.shape, BF16)
    dma = pltpu.SemaphoreType.DMA
    inputs = (
        pltpu.SMEM(row_order.shape, row_order.dtype),
        pltpu.SMEM(row_length.shape, row_length.dtype),
        pltpu.SMEM(amplitude.shape, F32),
        pltpu.VMEM((1, lat_total), row_order.dtype),
        pltpu.VMEM(control.shape, BF16),
        pltpu.VMEM(vertical.shape, BF16),
        pltpu.VMEM(meridional.shape, BF16),
        pltpu.VMEM(balance.shape, BF16),
    )
    balanced, basis = pl.pallas_call(
        functools.partial(blend_kernel, per_peer),
        name="blend",
        out_shape=(packed, table),
        in_specs=[anywhere] * 8,
        out_specs=(anywhere, anywhere),
        scratch_shapes=[
            *inputs,
            dma((8,)),
            seeds,
            seeds,
            table_vmem,
            pltpu.VMEM((levels, lons + LANES), BF16),
            block,
            block,
            pltpu.VMEM(packed.shape, F32),
            pltpu.VMEM((lat_total, per_peer * LANES), F32),
            pltpu.VMEM((lat_total, per_peer * LANES), BF16),
            block,
            pltpu.SemaphoreType.REGULAR,
            dma(()),
            dma(()),
            dma(()),
            dma(()),
            dma(()),
            dma((columns,)),
            dma(()),
            dma(()),
        ],
        compiler_params=pltpu.CompilerParams(collective_id=0, has_side_effects=True),
    )(
        row_order,
        row_length,
        amplitude,
        row_order.reshape(1, lat_total),
        control,
        vertical,
        meridional,
        balance,
    )
    return pl.pallas_call(
        functools.partial(synthesis_kernel, per_peer),
        name="synthesis",
        out_shape=jax.ShapeDtypeStruct(control.shape, BF16),
        in_specs=[anywhere] * 4,
        out_specs=anywhere,
        scratch_shapes=[
            inputs[0],
            inputs[1],
            block,
            pltpu.VMEM((levels, lons), BF16),
            table_vmem,
            pltpu.VMEM((levels, lons + LANES), F32),
            dma((11,)),
        ],
    )(row_order, row_length, balanced, basis)


def solution(mesh):
    return jax.shard_map(
        body,
        mesh=mesh,
        in_specs=(
            P("var", "lat", None, None),
            P(),
            P(),
            P("var", None, None),
            P("var", None),
            P("var", None, None),
            P("var", None, None),
        ),
        out_specs=P("var", "lat", None, None),
        check_vma=False,
    )
```

```python
import functools
import math

import jax
import jax.numpy as jnp
from jax import lax
from jax.experimental import pallas as pl
from jax.experimental.pallas import tpu as pltpu
from jax.sharding import PartitionSpec as P

LANES = 128
SUBS = 8
ROW = 16
F32 = jnp.float32
BF16 = jnp.bfloat16
MESH = pl.DeviceIdType.MESH


def iota(shape, dim):
    return lax.broadcasted_iota(jnp.int32, shape, dim)


def nt_dot(a, b):
    return lax.dot_general(a, b, (((1,), (1,)), ((), ())), preferred_element_type=F32)


def write_packed(ref, here, rows):
    for j in range(ref.shape[-1] // LANES):
        ref[here, :, pl.ds(j * LANES, LANES)] = rows[:, 2 * j : 2 * j + 2, :].astype(BF16)


def read_packed(ref, target_ref):
    for j in range(ref.shape[-1] // LANES):
        target_ref[:, pl.ds(2 * j, 2), :] = ref[:, :, pl.ds(j * LANES, LANES)].astype(F32)


def row_of(lat_total):
    return ROW if lat_total % ROW == 0 else 2


def far_first(count):
    return sorted(range(1, count), key=lambda step: -min(step, count - step))


def own_length(order_ref, length_ref):
    return length_ref[order_ref[lax.axis_index("lat")]]


def wave_seeds(period, cos_ref, sin_ref, groups, per_peer):
    shape = cos_ref.shape
    row = iota(shape, 0)
    local = row - groups
    fine = 4 * (local % SUBS) + local // SUBS
    wave = jnp.where(row < groups, 4 * per_peer * row, fine).astype(F32)
    phase = wave * iota(shape, 1).astype(F32)
    inverse = 1.0 / period
    phase = phase - jnp.floor(phase * inverse + 0.5) * period
    quadrant = jnp.floor(phase * (4.0 * inverse) + 0.5)
    angle = (4.0 * phase - quadrant * period) * inverse * (0.5 * math.pi)
    sq = angle * angle
    sine = angle * (1.0 + sq * (-1.0 / 6 + sq * (1.0 / 120 + sq * (-1.0 / 5040 + sq * (1.0 / 362880)))))
    cosine = 1.0 + sq * (-0.5 + sq * (1.0 / 24 + sq * (-1.0 / 720 + sq * (1.0 / 40320))))
    odd = jnp.abs(quadrant) == 1.0
    flip = jnp.abs(quadrant) == 2.0
    sign = jnp.where(flip, -1.0, jnp.where(odd, quadrant, 1.0))
    cos_ref[...] = jnp.where(odd, -sign * sine, sign * cosine)
    sin_ref[...] = jnp.where(odd, sign * cosine, sign * sine)


def fill_table(cos_ref, sin_ref, table_ref, groups):
    blocks = table_ref.shape[0] // 2
    rows = groups * SUBS

    def one(step, carry):
        rem, blk = step // blocks, step % blocks
        cols = pl.ds(pl.multiple_of(blk * LANES, LANES), LANES)
        fine = pl.ds(pl.multiple_of(groups + rem * SUBS, SUBS), SUBS)
        cos_f, sin_f = cos_ref[fine, cols], sin_ref[fine, cols]
        for group in range(0, groups, 2):
            cosine, sine = [], []
            for g in (group, group + 1):
                cos_c, sin_c = cos_ref[pl.ds(g, 1), cols], sin_ref[pl.ds(g, 1), cols]
                cosine.append(cos_c * cos_f - sin_c * sin_f)
                sine.append(sin_c * cos_f + cos_c * sin_f)
            dest = pl.ds(pl.multiple_of(rem * rows + group * SUBS, 2 * SUBS), 2 * SUBS)
            table_ref[blk, dest, :] = jnp.concatenate(cosine, axis=0).astype(BF16)
            table_ref[blk + blocks, dest, :] = jnp.concatenate(sine, axis=0).astype(BF16)
        return carry

    lax.fori_loop(0, 4 * blocks, one, 0)


def table_rows(table_ref, rem, rows, first, last):
    here = pl.ds(rem * rows, rows)
    return jnp.concatenate([table_ref[b, here, :] for b in range(first, last)], axis=1)


def row_wave(lat_total, per_peer):
    groups = lat_total // 4
    shape = (lat_total, SUBS, LANES)
    peer = iota(shape, 0)
    sub = iota(shape, 1)
    wave = 4 * (peer % groups * per_peer + sub) + peer // groups
    return wave, sub < per_peer


def analyse(length, per_peer, control_ref, vertical_ref, coeff_ref, table_ref, level_ref):
    lat_total = coeff_ref.shape[0]
    groups = lat_total // 4
    rows = groups * SUBS
    lons = control_ref.shape[-1]
    quarter = lons // 4
    blocks = quarter // LANES
    period = length.astype(F32)
    levels = jnp.dot(vertical_ref[0], control_ref[0, 0], preferred_element_type=F32)
    level_ref[:, pl.ds(0, lons)] = levels.astype(BF16)
    level_ref[:, pl.ds(lons, LANES)] = jnp.zeros((levels.shape[0], LANES), BF16)
    count = levels.shape[0]
    step = length // 4
    lane = iota((count, LANES), 1)
    columns = [level_ref[:, pl.ds(b * LANES, LANES)] for b in range(4 * blocks + 1)]

    def shifted(part):
        base = part * step
        start, shift = base // LANES, base % LANES
        held = columns
        bit = 1 << max(part * blocks, 1).bit_length() - 1
        while bit and part:
            moved = [held[c + bit] if c + bit < len(held) else held[c] for c in range(len(held))]
            set_here = start // bit % 2 == 1
            held = [jnp.where(set_here, m, h) for m, h in zip(moved, held)]
            held = held[: blocks + bit]
            bit //= 2
        pairs = [jnp.concatenate([held[b], held[b + 1]], axis=1) for b in range(blocks)]
        if part:
            turn = (2 * LANES, LANES)
            place = jnp.where(iota(turn, 0) == iota(turn, 1) + shift, 1.0, 0.0).astype(BF16)
            both = jnp.dot(jnp.concatenate(pairs, axis=0), place, preferred_element_type=F32)
            parts = [both[b * count : (b + 1) * count] for b in range(blocks)]
        else:
            parts = [held[b].astype(F32) for b in range(blocks)]
        return jnp.concatenate(
            [jnp.where(lane + b * LANES < step, parts[b], 0.0) for b in range(blocks)], axis=1
        )

    x0, x1, x2, x3 = (shifted(q) for q in range(4))
    y0 = ((x0 + x2) + (x1 + x3)).astype(BF16)
    y2 = ((x0 + x2) - (x1 + x3)).astype(BF16)
    a = (x0 - x2).astype(BF16)
    b = (x1 - x3).astype(BF16)
    zero = jnp.zeros_like(y0)
    weights = (
        ((y0, zero), (zero, y0)),
        ((a, -b), (b, a)),
        ((y2, zero), (zero, y2)),
        ((a, b), (-b, a)),
    )
    wave, held = row_wave(lat_total, per_peer)
    scale = jnp.where(wave == 0, 1.0, 2.0) / period
    scale = jnp.where(held & (wave <= (length - 1) // 2), scale, 0.0)
    for rem in range(4):
        upper, lower = weights[rem]
        mixed = jnp.concatenate(
            [jnp.concatenate(upper, axis=1), jnp.concatenate(lower, axis=1)], axis=0
        )
        part = nt_dot(table_rows(table_ref, rem, rows, 0, 2 * blocks), mixed)
        part = part.reshape(groups, SUBS, LANES) * scale[rem * groups : (rem + 1) * groups]
        write_packed(coeff_ref, pl.ds(rem * groups, groups), part)


def synthesis_kernel(
    per_peer,
    order_hbm,
    length_hbm,
    balanced_hbm,
    table_hbm,
    out_hbm,
    order_ref,
    length_ref,
    balanced_ref,
    spec_ref,
    out_ref,
    table_ref,
    wide_ref,
    sems,
):
    lat_total = balanced_ref.shape[0]
    arriving = [
        pltpu.make_async_copy(source, target, sems.at[4 + index])
        for index, (source, target) in enumerate(
            ((order_hbm, order_ref), (length_hbm, length_ref), (balanced_hbm, balanced_ref))
        )
    ]
    for copy in arriving:
        copy.start()
    groups = lat_total // 4
    rows = groups * SUBS
    count, lons = out_ref.shape[-2], out_ref.shape[-1]
    quarter = lons // 4
    blocks = quarter // LANES
    loads = []
    for rem in range(4):
        here = pl.ds(rem * rows, rows)
        loads.append(
            pltpu.make_async_copy(table_hbm.at[:, here], table_ref.at[:, here], sems.at[rem])
        )
        loads[-1].start()
    wide_ref[...] = jnp.zeros_like(wide_ref)
    arriving[0].wait()
    arriving[1].wait()
    length = own_length(order_ref, length_ref)
    arriving[2].wait()
    wave, held = row_wave(lat_total, per_peer)
    read_packed(balanced_ref, spec_ref)
    spectra = jnp.where(held & (wave <= (length - 1) // 2), spec_ref[...], 0.0)
    turned = spectra.reshape(lat_total * SUBS, LANES).T.astype(BF16)

    def parts(rem):
        both = turned[:, rem * rows : (rem + 1) * rows]
        return both[:count], both[count:]

    def against(rem, on_cos, on_sin):
        loads[rem].wait()
        return jnp.dot(
            on_cos, table_rows(table_ref, rem, rows, 0, blocks), preferred_element_type=F32
        ) + jnp.dot(
            on_sin, table_rows(table_ref, rem, rows, blocks, 2 * blocks), preferred_element_type=F32
        )

    c0, s0 = parts(0)
    c1, s1 = parts(1)
    c2, s2 = parts(2)
    c3, s3 = parts(3)
    e0 = against(0, c0, s0)
    e2 = against(2, c2, s2)
    ab = against(
        1, jnp.concatenate([c1, s1], axis=0), jnp.concatenate([s1, -c1], axis=0)
    ) + against(3, jnp.concatenate([c3, -s3], axis=0), jnp.concatenate([s3, c3], axis=0))
    a, b = ab[:count], ab[count:]
    step = length // 4
    lane = iota((count, LANES), 1)
    for part, piece in enumerate(((e0 + e2) + a, (e0 - e2) + b, (e0 + e2) - a, (e0 - e2) - b)):
        base = part * step
        start = base // LANES
        shift = base % LANES
        before = jnp.zeros((count, LANES), F32)
        for blk in range(blocks + 1):
            if blk < blocks:
                own = piece[:, blk * LANES : (blk + 1) * LANES]
                own = jnp.where(lane + blk * LANES < step, own, 0.0)
                rolled = pltpu.roll(own, shift, 1)
            else:
                rolled = jnp.zeros((count, LANES), F32)
            here = pl.ds(pl.multiple_of((start + blk) * LANES, LANES), LANES)
            wide_ref[:, here] += jnp.where(lane >= shift, rolled, before)
            before = rolled
    leaving = []
    for part in range(4):
        here = pl.ds(part * quarter, quarter)
        out_ref[:, here] = wide_ref[:, here].astype(BF16)
        leaving.append(
            pltpu.make_async_copy(out_ref.at[:, here], out_hbm.at[0, 0, :, here], sems.at[7 + part])
        )
        leaving[-1].start()
    for copy in leaving:
        copy.wait()


def blend_kernel(
    per_peer,
    order_hbm,
    length_hbm,
    amp_hbm,
    order_row_hbm,
    control_hbm,
    vertical_hbm,
    meridional_hbm,
    balance_hbm,
    balanced_hbm,
    table_hbm,
    order_smem,
    length_ref,
    amp_ref,
    order_ref,
    control_ref,
    vertical_ref,
    meridional_ref,
    balance_ref,
    input_sems,
    cos_ref,
    sin_ref,
    table_ref,
    level_ref,
    coeff_ref,
    recv_ref,
    wide_ref,
    product_ref,
    root_ref,
    mixed_ref,
    line_sem,
    table_sem,
    local_sem,
    send_sem,
    recv_sem,
    root_send_sem,
    root_recv_sem,
    back_send_sem,
    back_recv_sem,
):
    lat_total = balanced_hbm.shape[0]
    groups = lat_total // 4
    me = lax.axis_index("lat")
    var = lax.axis_index("var")
    var_total = lax.axis_size("var")
    row_size = row_of(lat_total)
    columns = lat_total // row_size
    line, place = lax.div(me, row_size), lax.rem(me, row_size)
    barrier = pltpu.get_barrier_semaphore()
    arriving = []
    for index, (source, target) in enumerate(
        (
            (order_hbm, order_smem),
            (length_hbm, length_ref),
            (vertical_hbm, vertical_ref),
            (control_hbm, control_ref),
            (amp_hbm, amp_ref),
            (order_row_hbm, order_ref),
            (meridional_hbm, meridional_ref),
            (balance_hbm, balance_ref),
        )
    ):
        arriving.append(pltpu.make_async_copy(source, target, input_sems.at[index]))

    def greet(sem, **where):
        pl.semaphore_signal(sem, 1, device_id=where, device_id_type=MESH)

    def greet_column(sem):
        for step in far_first(columns):
            greet(sem, lat=lax.rem(line + step, columns) * row_size + place)

    arriving[0].start()
    arriving[1].start()
    for step in far_first(row_size):
        greet(barrier, lat=line * row_size + lax.rem(place + step, row_size))
    greet_column(barrier)
    for step in range(1, var_total):
        greet(barrier, var=lax.rem(var + step, var_total))
    for copy in arriving[2:]:
        copy.start()

    arriving[0].wait()
    arriving[1].wait()
    length = own_length(order_smem, length_ref)
    wave_seeds(length.astype(F32), cos_ref, sin_ref, groups, per_peer)
    fill_table(cos_ref, sin_ref, table_ref, groups)
    table_copy = pltpu.make_async_copy(table_ref, table_hbm, table_sem)
    table_copy.start()
    pl.semaphore_wait(barrier, row_size - 1 + columns - 1 + var_total - 1)
    greet_column(line_sem)
    arriving[2].wait()
    arriving[3].wait()
    analyse(length, per_peer, control_ref, vertical_ref, coeff_ref, table_ref, level_ref)
    pl.semaphore_wait(line_sem, columns - 1)

    def to_peer(src_ref, dst_ref, peer, src_sem, dst_sem):
        return pltpu.make_async_remote_copy(
            src_ref=src_ref.at[peer],
            dst_ref=dst_ref.at[me],
            send_sem=src_sem,
            recv_sem=dst_sem,
            device_id={"lat": peer},
            device_id_type=MESH,
        )

    def to_line(there, src_ref, dst_ref, src_sem, dst_sem, own=None):
        def one(offset, carry):
            peer = there * row_size + lax.rem(place + offset, row_size)

            def start():
                to_peer(src_ref, dst_ref, peer, src_sem, dst_sem).start()

            if own is None:
                pl.when(peer != me)(start)
            else:
                start()
            return carry

        lax.fori_loop(1 if own else 0, row_size, one, 0, unroll=True)

    def first(there, own=False):
        to_line(there, coeff_ref, recv_ref, send_sem, recv_sem, own)

    def send(step, carry):
        first(lax.rem(line + columns // 2 + step, columns))
        first(lax.rem(line + columns // 2 - step, columns))
        return carry

    first(lax.rem(line + columns // 2, columns))
    lax.fori_loop(1, columns // 2, send, 0)
    first(line, own=True)
    own = pltpu.make_async_copy(coeff_ref.at[me], recv_ref.at[me], local_sem)
    own.start()
    for copy in arriving[4:]:
        copy.wait()
    pick = jnp.where(iota((lat_total, lat_total), 0) == order_ref[...], 1.0, 0.0).astype(BF16)
    slot_mat = jnp.dot(meridional_ref[0], pick, preferred_element_type=F32).astype(BF16)
    slot_mat = lax.dot_general(
        pick, slot_mat, (((0,), (0,)), ((), ())), preferred_element_type=F32
    ).astype(BF16)
    block = balance_ref[0]
    none = jnp.zeros_like(block)
    lift = jnp.concatenate(
        [jnp.concatenate([block, none], axis=1), jnp.concatenate([none, block], axis=1)], axis=0
    )
    own.wait()
    rest = pl.ds(0, lat_total - 1)

    def settle(ref, sem):
        pltpu.make_async_copy(ref.at[rest], ref.at[rest], sem).wait()

    settle(recv_ref, recv_sem)
    read_packed(recv_ref, wide_ref)
    received = [wide_ref[:, sub, :].astype(BF16) for sub in range(per_peer)]
    product = jnp.dot(slot_mat, jnp.concatenate(received, axis=1), preferred_element_type=F32)
    scaled = []
    for sub in range(per_peer):
        wave = 4 * (me % groups * per_peer + sub) + me // groups
        scaled.append(product[:, sub * LANES : (sub + 1) * LANES] * amp_ref[0, wave])
    product_ref[...] = jnp.concatenate(scaled, axis=1)

    def piece_rows(piece):
        there = lax.rem(line + columns // 2 + piece, columns)
        return there, pl.ds(pl.multiple_of(there * row_size, row_size), row_size)

    def root_copy(piece, target):
        _, here = piece_rows(piece)
        return pltpu.make_async_remote_copy(
            src_ref=root_ref.at[here],
            dst_ref=root_ref.at[here],
            send_sem=root_send_sem,
            recv_sem=root_recv_sem.at[piece],
            device_id={"var": target},
            device_id_type=MESH,
        )

    half = columns // 2
    relayed = var_total == 4

    @pl.when(var == 0)
    def _():
        root_ref[...] = product_ref[...].astype(BF16)
        for step in range(columns):
            if relayed:
                root_copy(step, 1).start()
                root_copy(columns - 1 - step, 3).start()
            else:
                for target in range(1, var_total):
                    root_copy(step, target).start()

    def await_root(piece):
        _, here = piece_rows(piece)
        pltpu.make_async_copy(root_ref.at[here], root_ref.at[here], root_recv_sem.at[piece]).wait()

    def relay(step):
        piece = jnp.where(var == 1, step, columns - 1 - step)
        await_root(piece)
        root_copy(piece, 2).start()

    between = (var == 1) | (var == 3)
    if relayed:
        pl.when(between)(lambda: relay(0))

    def one_piece(step, carry):
        outside_in = jnp.where(step % 2 == 0, step // 2, columns - 1 - step // 2)
        piece = jnp.where(var == 1, step, jnp.where(var == 3, columns - 1 - step, outside_in))
        there, here = piece_rows(piece)
        if relayed:
            pl.when(between & (step + 1 < half))(lambda: relay(step + 1))

        waiting = var > 0
        if relayed:
            passed_on = ((var == 1) & (piece < half)) | ((var == 3) & (piece >= half))
            waiting = waiting & jnp.logical_not(passed_on)

        @pl.when(waiting)
        def _():
            await_root(piece)

        part = root_ref[here, :]
        stacked = jnp.concatenate(
            [part[:, sub * LANES : (sub + 1) * LANES] for sub in range(per_peer)], axis=0
        )
        lifted = nt_dot(stacked, lift)
        for sub in range(per_peer):
            blended = product_ref[here, pl.ds(sub * LANES, LANES)]
            addend = lifted[sub * row_size : (sub + 1) * row_size]
            wide_ref[here, sub, :] = blended + jnp.where(var > 0, addend, 0.0)
        write_packed(mixed_ref, here, wide_ref[here])

        to_line(there, mixed_ref, balanced_hbm, back_send_sem, back_recv_sem)
        return carry

    lax.fori_loop(0, columns, one_piece, 0)
    own = pltpu.make_async_copy(mixed_ref.at[me], balanced_hbm.at[me], local_sem)
    own.start()
    own.wait()
    table_copy.wait()
    settle(coeff_ref, send_sem)

    def sent_roots(pieces):
        span = pl.ds(0, pieces * row_size)
        pltpu.make_async_copy(root_ref.at[span], root_ref.at[span], root_send_sem).wait()

    @pl.when(var == 0)
    def _():
        for _ in range(2 if relayed else var_total - 1):
            sent_roots(columns)

    if relayed:

        @pl.when(between)
        def _():
            sent_roots(half)

    settle(mixed_ref, back_send_sem)
    settle(balanced_hbm, back_recv_sem)


def body(control, row_order, row_length, vertical, amplitude, meridional, balance):
    lat_total = row_order.shape[0]
    levels, lons = control.shape[2:]
    waves = amplitude.shape[1]
    per_peer = waves // lat_total
    groups = lat_total // 4
    quarter = lons // 4
    blocks = quarter // LANES
    columns = lat_total // row_of(lat_total)
    anywhere = pl.BlockSpec(memory_space=pl.ANY)
    seeds = pltpu.VMEM((groups + 4 * SUBS, quarter), F32)
    packed = jax.ShapeDtypeStruct((lat_total, 2, per_peer // 2 * LANES), BF16)
    table = jax.ShapeDtypeStruct((2 * blocks, lat_total * SUBS, LANES), BF16)
    table_vmem = pltpu.VMEM(table.shape, BF16)
    block = pltpu.VMEM(packed.shape, BF16)
    dma = pltpu.SemaphoreType.DMA
    inputs = (
        pltpu.SMEM(row_order.shape, row_order.dtype),
        pltpu.SMEM(row_length.shape, row_length.dtype),
        pltpu.SMEM(amplitude.shape, F32),
        pltpu.VMEM((1, lat_total), row_order.dtype),
        pltpu.VMEM(control.shape, BF16),
        pltpu.VMEM(vertical.shape, BF16),
        pltpu.VMEM(meridional.shape, BF16),
        pltpu.VMEM(balance.shape, BF16),
    )
    balanced, basis = pl.pallas_call(
        functools.partial(blend_kernel, per_peer),
        name="blend",
        out_shape=(packed, table),
        in_specs=[anywhere] * 8,
        out_specs=(anywhere, anywhere),
        scratch_shapes=[
            *inputs,
            dma((8,)),
            seeds,
            seeds,
            table_vmem,
            pltpu.VMEM((levels, lons + LANES), BF16),
            block,
            block,
            pltpu.VMEM((lat_total, SUBS, LANES), F32),
            pltpu.VMEM((lat_total, per_peer * LANES), F32),
            pltpu.VMEM((lat_total, per_peer * LANES), BF16),
            block,
            pltpu.SemaphoreType.REGULAR,
            dma(()),
            dma(()),
            dma(()),
            dma(()),
            dma(()),
            dma((columns,)),
            dma(()),
            dma(()),
        ],
        compiler_params=pltpu.CompilerParams(collective_id=0, has_side_effects=True),
    )(
        row_order,
        row_length,
        amplitude,
        row_order.reshape(1, lat_total),
        control,
        vertical,
        meridional,
        balance,
    )
    return pl.pallas_call(
        functools.partial(synthesis_kernel, per_peer),
        name="synthesis",
        out_shape=jax.ShapeDtypeStruct(control.shape, BF16),
        in_specs=[anywhere] * 4,
        out_specs=anywhere,
        scratch_shapes=[
            inputs[0],
            inputs[1],
            block,
            pltpu.VMEM((lat_total, SUBS, LANES), F32),
            pltpu.VMEM((levels, lons), BF16),
            table_vmem,
            pltpu.VMEM((levels, lons + LANES), F32),
            dma((11,)),
        ],
    )(row_order, row_length, balanced, basis)


def solution(mesh):
    return jax.shard_map(
        body,
        mesh=mesh,
        in_specs=(
            P("var", "lat", None, None),
            P(),
            P(),
            P("var", None, None),
            P("var", None),
            P("var", None, None),
            P("var", None, None),
        ),
        out_specs=P("var", "lat", None, None),
        check_vma=False,
    )
```

```python
import functools
import math

import jax
import jax.numpy as jnp
from jax import lax
from jax.experimental import pallas as pl
from jax.experimental.pallas import tpu as pltpu
from jax.sharding import PartitionSpec as P

LANES = 128
SUBS = 8
ROW = 16
F32 = jnp.float32
BF16 = jnp.bfloat16
MESH = pl.DeviceIdType.MESH


def iota(shape, dim):
    return lax.broadcasted_iota(jnp.int32, shape, dim)


def nt_dot(a, b):
    return lax.dot_general(a, b, (((1,), (1,)), ((), ())), preferred_element_type=F32)


def write_packed(ref, here, rows):
    for j in range(ref.shape[-1] // LANES):
        ref[here, :, pl.ds(j * LANES, LANES)] = rows[:, 2 * j : 2 * j + 2, :].astype(BF16)


def read_packed(ref, target_ref):
    for j in range(ref.shape[-1] // LANES):
        target_ref[:, pl.ds(2 * j, 2), :] = ref[:, :, pl.ds(j * LANES, LANES)].astype(F32)


def row_of(lat_total):
    return ROW if lat_total % ROW == 0 else 2


def far_first(count):
    return sorted(range(1, count), key=lambda step: -min(step, count - step))


def own_length(order_ref, length_ref):
    return length_ref[order_ref[lax.axis_index("lat")]]


def wave_seeds(period, cos_ref, sin_ref, groups, per_peer):
    shape = cos_ref.shape
    row = iota(shape, 0)
    local = row - groups
    fine = 4 * (local % SUBS) + local // SUBS
    wave = jnp.where(row < groups, 4 * per_peer * row, fine).astype(F32)
    phase = wave * iota(shape, 1).astype(F32)
    inverse = 1.0 / period
    phase = phase - jnp.floor(phase * inverse + 0.5) * period
    quadrant = jnp.floor(phase * (4.0 * inverse) + 0.5)
    angle = (4.0 * phase - quadrant * period) * inverse * (0.5 * math.pi)
    sq = angle * angle
    sine = angle * (1.0 + sq * (-1.0 / 6 + sq * (1.0 / 120 + sq * (-1.0 / 5040 + sq * (1.0 / 362880)))))
    cosine = 1.0 + sq * (-0.5 + sq * (1.0 / 24 + sq * (-1.0 / 720 + sq * (1.0 / 40320))))
    odd = jnp.abs(quadrant) == 1.0
    flip = jnp.abs(quadrant) == 2.0
    sign = jnp.where(flip, -1.0, jnp.where(odd, quadrant, 1.0))
    cos_ref[...] = jnp.where(odd, -sign * sine, sign * cosine)
    sin_ref[...] = jnp.where(odd, sign * cosine, sign * sine)


def fill_table(cos_ref, sin_ref, table_ref, groups):
    blocks = table_ref.shape[0] // 2
    rows = groups * SUBS

    def one(step, carry):
        rem, blk = step // blocks, step % blocks
        cols = pl.ds(pl.multiple_of(blk * LANES, LANES), LANES)
        fine = pl.ds(pl.multiple_of(groups + rem * SUBS, SUBS), SUBS)
        cos_f, sin_f = cos_ref[fine, cols], sin_ref[fine, cols]
        for group in range(0, groups, 2):
            cosine, sine = [], []
            for g in (group, group + 1):
                cos_c, sin_c = cos_ref[pl.ds(g, 1), cols], sin_ref[pl.ds(g, 1), cols]
                cosine.append(cos_c * cos_f - sin_c * sin_f)
                sine.append(sin_c * cos_f + cos_c * sin_f)
            dest = pl.ds(pl.multiple_of(rem * rows + group * SUBS, 2 * SUBS), 2 * SUBS)
            table_ref[blk, dest, :] = jnp.concatenate(cosine, axis=0).astype(BF16)
            table_ref[blk + blocks, dest, :] = jnp.concatenate(sine, axis=0).astype(BF16)
        return carry

    lax.fori_loop(0, 4 * blocks, one, 0)


def table_rows(table_ref, rem, rows, first, last):
    here = pl.ds(rem * rows, rows)
    return jnp.concatenate([table_ref[b, here, :] for b in range(first, last)], axis=1)


def row_wave(lat_total, per_peer):
    groups = lat_total // 4
    shape = (lat_total, SUBS, LANES)
    peer = iota(shape, 0)
    sub = iota(shape, 1)
    wave = 4 * (peer % groups * per_peer + sub) + peer // groups
    return wave, sub < per_peer


def analyse(length, per_peer, control_ref, vertical_ref, coeff_ref, table_ref, level_ref):
    lat_total = coeff_ref.shape[0]
    groups = lat_total // 4
    rows = groups * SUBS
    lons = control_ref.shape[-1]
    quarter = lons // 4
    blocks = quarter // LANES
    period = length.astype(F32)
    levels = jnp.dot(vertical_ref[0], control_ref[0, 0], preferred_element_type=F32)
    level_ref[:, pl.ds(0, lons)] = levels.astype(BF16)
    level_ref[:, pl.ds(lons, LANES)] = jnp.zeros((levels.shape[0], LANES), BF16)
    count = levels.shape[0]
    step = length // 4
    lane = iota((count, LANES), 1)
    columns = [level_ref[:, pl.ds(b * LANES, LANES)] for b in range(4 * blocks + 1)]

    def shifted(part):
        base = part * step
        start, shift = base // LANES, base % LANES
        held = columns
        bit = 1 << max(part * blocks, 1).bit_length() - 1
        while bit and part:
            moved = [held[c + bit] if c + bit < len(held) else held[c] for c in range(len(held))]
            set_here = start // bit % 2 == 1
            held = [jnp.where(set_here, m, h) for m, h in zip(moved, held)]
            held = held[: blocks + bit]
            bit //= 2
        pairs = [jnp.concatenate([held[b], held[b + 1]], axis=1) for b in range(blocks)]
        if part:
            turn = (2 * LANES, LANES)
            place = jnp.where(iota(turn, 0) == iota(turn, 1) + shift, 1.0, 0.0).astype(BF16)
            both = jnp.dot(jnp.concatenate(pairs, axis=0), place, preferred_element_type=F32)
            parts = [both[b * count : (b + 1) * count] for b in range(blocks)]
        else:
            parts = [held[b].astype(F32) for b in range(blocks)]
        return jnp.concatenate(
            [jnp.where(lane + b * LANES < step, parts[b], 0.0) for b in range(blocks)], axis=1
        )

    x0, x1, x2, x3 = (shifted(q) for q in range(4))
    y0 = ((x0 + x2) + (x1 + x3)).astype(BF16)
    y2 = ((x0 + x2) - (x1 + x3)).astype(BF16)
    a = (x0 - x2).astype(BF16)
    b = (x1 - x3).astype(BF16)
    zero = jnp.zeros_like(y0)
    weights = (
        ((y0, zero), (zero, y0)),
        ((a, -b), (b, a)),
        ((y2, zero), (zero, y2)),
        ((a, b), (-b, a)),
    )
    wave, held = row_wave(lat_total, per_peer)
    scale = jnp.where(wave == 0, 1.0, 2.0) / period
    scale = jnp.where(held & (wave <= (length - 1) // 2), scale, 0.0)
    for rem in range(4):
        upper, lower = weights[rem]
        mixed = jnp.concatenate(
            [jnp.concatenate(upper, axis=1), jnp.concatenate(lower, axis=1)], axis=0
        )
        part = nt_dot(table_rows(table_ref, rem, rows, 0, 2 * blocks), mixed)
        part = part.reshape(groups, SUBS, LANES) * scale[rem * groups : (rem + 1) * groups]
        write_packed(coeff_ref, pl.ds(rem * groups, groups), part)


def synthesis_kernel(
    per_peer,
    order_hbm,
    length_hbm,
    balanced_hbm,
    table_hbm,
    out_hbm,
    order_ref,
    length_ref,
    balanced_ref,
    spec_ref,
    out_ref,
    table_ref,
    wide_ref,
    sems,
):
    lat_total = balanced_ref.shape[0]
    arriving = [
        pltpu.make_async_copy(source, target, sems.at[4 + index])
        for index, (source, target) in enumerate(
            ((order_hbm, order_ref), (length_hbm, length_ref), (balanced_hbm, balanced_ref))
        )
    ]
    for copy in arriving:
        copy.start()
    groups = lat_total // 4
    rows = groups * SUBS
    count, lons = out_ref.shape[-2], out_ref.shape[-1]
    quarter = lons // 4
    blocks = quarter // LANES
    loads = []
    for rem in range(4):
        here = pl.ds(rem * rows, rows)
        loads.append(
            pltpu.make_async_copy(table_hbm.at[:, here], table_ref.at[:, here], sems.at[rem])
        )
        loads[-1].start()
    wide_ref[...] = jnp.zeros_like(wide_ref)
    arriving[0].wait()
    arriving[1].wait()
    length = own_length(order_ref, length_ref)
    arriving[2].wait()
    wave, held = row_wave(lat_total, per_peer)
    read_packed(balanced_ref, spec_ref)
    spectra = jnp.where(held & (wave <= (length - 1) // 2), spec_ref[...], 0.0)
    turned = spectra.reshape(lat_total * SUBS, LANES).T.astype(BF16)

    def parts(rem):
        both = turned[:, rem * rows : (rem + 1) * rows]
        return both[:count], both[count:]

    def against(rem, on_cos, on_sin):
        loads[rem].wait()
        return jnp.dot(
            on_cos, table_rows(table_ref, rem, rows, 0, blocks), preferred_element_type=F32
        ) + jnp.dot(
            on_sin, table_rows(table_ref, rem, rows, blocks, 2 * blocks), preferred_element_type=F32
        )

    c0, s0 = parts(0)
    c1, s1 = parts(1)
    c2, s2 = parts(2)
    c3, s3 = parts(3)
    e0 = against(0, c0, s0)
    e2 = against(2, c2, s2)
    ab = against(
        1, jnp.concatenate([c1, s1], axis=0), jnp.concatenate([s1, -c1], axis=0)
    ) + against(3, jnp.concatenate([c3, -s3], axis=0), jnp.concatenate([s3, c3], axis=0))
    a, b = ab[:count], ab[count:]
    step = length // 4
    lane = iota((count, LANES), 1)
    for part, piece in enumerate(((e0 + e2) + a, (e0 - e2) + b, (e0 + e2) - a, (e0 - e2) - b)):
        base = part * step
        start = base // LANES
        shift = base % LANES
        before = jnp.zeros((count, LANES), F32)
        for blk in range(blocks + 1):
            if blk < blocks:
                own = piece[:, blk * LANES : (blk + 1) * LANES]
                own = jnp.where(lane + blk * LANES < step, own, 0.0)
                rolled = pltpu.roll(own, shift, 1)
            else:
                rolled = jnp.zeros((count, LANES), F32)
            here = pl.ds(pl.multiple_of((start + blk) * LANES, LANES), LANES)
            wide_ref[:, here] += jnp.where(lane >= shift, rolled, before)
            before = rolled
    leaving = []
    for part in range(4):
        here = pl.ds(part * quarter, quarter)
        out_ref[:, here] = wide_ref[:, here].astype(BF16)
        leaving.append(
            pltpu.make_async_copy(out_ref.at[:, here], out_hbm.at[0, 0, :, here], sems.at[7 + part])
        )
        leaving[-1].start()
    for copy in leaving:
        copy.wait()


def blend_kernel(
    per_peer,
    order_hbm,
    length_hbm,
    amp_hbm,
    order_row_hbm,
    control_hbm,
    vertical_hbm,
    meridional_hbm,
    balance_hbm,
    balanced_hbm,
    table_hbm,
    order_smem,
    length_ref,
    amp_ref,
    order_ref,
    control_ref,
    vertical_ref,
    meridional_ref,
    balance_ref,
    input_sems,
    cos_ref,
    sin_ref,
    table_ref,
    level_ref,
    coeff_ref,
    recv_ref,
    wide_ref,
    product_ref,
    root_ref,
    mixed_ref,
    line_sem,
    table_sem,
    local_sem,
    send_sem,
    recv_sem,
    root_send_sem,
    root_recv_sem,
    back_send_sem,
    back_recv_sem,
):
    lat_total = balanced_hbm.shape[0]
    groups = lat_total // 4
    me = lax.axis_index("lat")
    var = lax.axis_index("var")
    var_total = lax.axis_size("var")
    row_size = row_of(lat_total)
    columns = lat_total // row_size
    line, place = lax.div(me, row_size), lax.rem(me, row_size)
    barrier = pltpu.get_barrier_semaphore()
    arriving = []
    for index, (source, target) in enumerate(
        (
            (order_hbm, order_smem),
            (length_hbm, length_ref),
            (vertical_hbm, vertical_ref),
            (control_hbm, control_ref),
            (amp_hbm, amp_ref),
            (order_row_hbm, order_ref),
            (meridional_hbm, meridional_ref),
            (balance_hbm, balance_ref),
        )
    ):
        arriving.append(pltpu.make_async_copy(source, target, input_sems.at[index]))

    def greet(sem, **where):
        pl.semaphore_signal(sem, 1, device_id=where, device_id_type=MESH)

    def greet_column(sem):
        for step in far_first(columns):
            greet(sem, lat=lax.rem(line + step, columns) * row_size + place)

    arriving[0].start()
    arriving[1].start()
    for step in far_first(row_size):
        greet(barrier, lat=line * row_size + lax.rem(place + step, row_size))
    greet_column(barrier)
    for step in range(1, var_total):
        greet(barrier, var=lax.rem(var + step, var_total))
    for copy in arriving[2:]:
        copy.start()

    arriving[0].wait()
    arriving[1].wait()
    length = own_length(order_smem, length_ref)
    wave_seeds(length.astype(F32), cos_ref, sin_ref, groups, per_peer)
    fill_table(cos_ref, sin_ref, table_ref, groups)
    table_copy = pltpu.make_async_copy(table_ref, table_hbm, table_sem)
    table_copy.start()
    pl.semaphore_wait(barrier, row_size - 1 + columns - 1 + var_total - 1)
    greet_column(line_sem)
    arriving[2].wait()
    arriving[3].wait()
    analyse(length, per_peer, control_ref, vertical_ref, coeff_ref, table_ref, level_ref)
    pl.semaphore_wait(line_sem, columns - 1)

    def to_peer(src_ref, dst_ref, peer, src_sem, dst_sem):
        return pltpu.make_async_remote_copy(
            src_ref=src_ref.at[peer],
            dst_ref=dst_ref.at[me],
            send_sem=src_sem,
            recv_sem=dst_sem,
            device_id={"lat": peer},
            device_id_type=MESH,
        )

    def to_line(there, src_ref, dst_ref, src_sem, dst_sem, own=None):
        def one(offset, carry):
            peer = there * row_size + lax.rem(place + offset, row_size)

            def start():
                to_peer(src_ref, dst_ref, peer, src_sem, dst_sem).start()

            if own is None:
                pl.when(peer != me)(start)
            else:
                start()
            return carry

        lax.fori_loop(1 if own else 0, row_size, one, 0, unroll=True)

    def first(there, own=False):
        to_line(there, coeff_ref, recv_ref, send_sem, recv_sem, own)

    def send(step, carry):
        first(lax.rem(line + columns // 2 + step, columns))
        first(lax.rem(line + columns // 2 - step, columns))
        return carry

    first(lax.rem(line + columns // 2, columns))
    lax.fori_loop(1, columns // 2, send, 0)
    first(line, own=True)
    own = pltpu.make_async_copy(coeff_ref.at[me], recv_ref.at[me], local_sem)
    own.start()
    for copy in arriving[4:]:
        copy.wait()
    pick = jnp.where(iota((lat_total, lat_total), 0) == order_ref[...], 1.0, 0.0).astype(BF16)
    slot_mat = jnp.dot(meridional_ref[0], pick, preferred_element_type=F32).astype(BF16)
    slot_mat = lax.dot_general(
        pick, slot_mat, (((0,), (0,)), ((), ())), preferred_element_type=F32
    ).astype(BF16)
    block = balance_ref[0]
    none = jnp.zeros_like(block)
    lift = jnp.concatenate(
        [jnp.concatenate([block, none], axis=1), jnp.concatenate([none, block], axis=1)], axis=0
    )
    own.wait()
    rest = pl.ds(0, lat_total - 1)

    def settle(ref, sem):
        pltpu.make_async_copy(ref.at[rest], ref.at[rest], sem).wait()

    settle(recv_ref, recv_sem)
    read_packed(recv_ref, wide_ref)
    received = [wide_ref[:, sub, :].astype(BF16) for sub in range(per_peer)]
    product = jnp.dot(slot_mat, jnp.concatenate(received, axis=1), preferred_element_type=F32)
    scaled = []
    for sub in range(per_peer):
        wave = 4 * (me % groups * per_peer + sub) + me // groups
        scaled.append(product[:, sub * LANES : (sub + 1) * LANES] * amp_ref[0, wave])
    product_ref[...] = jnp.concatenate(scaled, axis=1)

    def piece_rows(piece):
        there = lax.rem(line + columns // 2 + piece, columns)
        return there, pl.ds(pl.multiple_of(there * row_size, row_size), row_size)

    def root_copy(piece, target):
        _, here = piece_rows(piece)
        return pltpu.make_async_remote_copy(
            src_ref=root_ref.at[here],
            dst_ref=root_ref.at[here],
            send_sem=root_send_sem,
            recv_sem=root_recv_sem.at[piece],
            device_id={"var": target},
            device_id_type=MESH,
        )

    half = columns // 2
    relayed = var_total == 4

    @pl.when(var == 0)
    def _():
        root_ref[...] = product_ref[...].astype(BF16)
        for step in range(columns):
            if relayed:
                root_copy(step, 1).start()
                root_copy(columns - 1 - step, 3).start()
            else:
                for target in range(1, var_total):
                    root_copy(step, target).start()

    def await_root(piece):
        _, here = piece_rows(piece)
        pltpu.make_async_copy(root_ref.at[here], root_ref.at[here], root_recv_sem.at[piece]).wait()

    def relay(step):
        piece = jnp.where(var == 1, step, columns - 1 - step)
        await_root(piece)
        root_copy(piece, 2).start()

    between = (var == 1) | (var == 3)
    if relayed:
        @pl.when(between)
        def _():
            relay(0)
            relay(1)


    def one_piece(step, carry):
        outside_in = jnp.where(step % 2 == 0, step // 2, columns - 1 - step // 2)
        piece = jnp.where(var == 1, step, jnp.where(var == 3, columns - 1 - step, outside_in))
        there, here = piece_rows(piece)
        if relayed:
            pl.when(between & (step + 2 < half))(lambda: relay(step + 2))

        waiting = var > 0
        if relayed:
            passed_on = ((var == 1) & (piece < half)) | ((var == 3) & (piece >= half))
            waiting = waiting & jnp.logical_not(passed_on)

        @pl.when(waiting)
        def _():
            await_root(piece)

        part = root_ref[here, :]
        stacked = jnp.concatenate(
            [part[:, sub * LANES : (sub + 1) * LANES] for sub in range(per_peer)], axis=0
        )
        lifted = nt_dot(stacked, lift)
        for sub in range(per_peer):
            blended = product_ref[here, pl.ds(sub * LANES, LANES)]
            addend = lifted[sub * row_size : (sub + 1) * row_size]
            wide_ref[here, sub, :] = blended + jnp.where(var > 0, addend, 0.0)
        write_packed(mixed_ref, here, wide_ref[here])

        to_line(there, mixed_ref, balanced_hbm, back_send_sem, back_recv_sem)
        return carry

    lax.fori_loop(0, columns, one_piece, 0)
    own = pltpu.make_async_copy(mixed_ref.at[me], balanced_hbm.at[me], local_sem)
    own.start()
    own.wait()
    table_copy.wait()
    settle(coeff_ref, send_sem)

    def sent_roots(pieces):
        span = pl.ds(0, pieces * row_size)
        pltpu.make_async_copy(root_ref.at[span], root_ref.at[span], root_send_sem).wait()

    @pl.when(var == 0)
    def _():
        for _ in range(2 if relayed else var_total - 1):
            sent_roots(columns)

    if relayed:

        @pl.when(between)
        def _():
            sent_roots(half)

    settle(mixed_ref, back_send_sem)
    settle(balanced_hbm, back_recv_sem)


def body(control, row_order, row_length, vertical, amplitude, meridional, balance):
    lat_total = row_order.shape[0]
    levels, lons = control.shape[2:]
    waves = amplitude.shape[1]
    per_peer = waves // lat_total
    groups = lat_total // 4
    quarter = lons // 4
    blocks = quarter // LANES
    columns = lat_total // row_of(lat_total)
    anywhere = pl.BlockSpec(memory_space=pl.ANY)
    seeds = pltpu.VMEM((groups + 4 * SUBS, quarter), F32)
    packed = jax.ShapeDtypeStruct((lat_total, 2, per_peer // 2 * LANES), BF16)
    table = jax.ShapeDtypeStruct((2 * blocks, lat_total * SUBS, LANES), BF16)
    table_vmem = pltpu.VMEM(table.shape, BF16)
    block = pltpu.VMEM(packed.shape, BF16)
    dma = pltpu.SemaphoreType.DMA
    inputs = (
        pltpu.SMEM(row_order.shape, row_order.dtype),
        pltpu.SMEM(row_length.shape, row_length.dtype),
        pltpu.SMEM(amplitude.shape, F32),
        pltpu.VMEM((1, lat_total), row_order.dtype),
        pltpu.VMEM(control.shape, BF16),
        pltpu.VMEM(vertical.shape, BF16),
        pltpu.VMEM(meridional.shape, BF16),
        pltpu.VMEM(balance.shape, BF16),
    )
    balanced, basis = pl.pallas_call(
        functools.partial(blend_kernel, per_peer),
        name="blend",
        out_shape=(packed, table),
        in_specs=[anywhere] * 8,
        out_specs=(anywhere, anywhere),
        scratch_shapes=[
            *inputs,
            dma((8,)),
            seeds,
            seeds,
            table_vmem,
            pltpu.VMEM((levels, lons + LANES), BF16),
            block,
            block,
            pltpu.VMEM((lat_total, SUBS, LANES), F32),
            pltpu.VMEM((lat_total, per_peer * LANES), F32),
            pltpu.VMEM((lat_total, per_peer * LANES), BF16),
            block,
            pltpu.SemaphoreType.REGULAR,
            dma(()),
            dma(()),
            dma(()),
            dma(()),
            dma(()),
            dma((columns,)),
            dma(()),
            dma(()),
        ],
        compiler_params=pltpu.CompilerParams(collective_id=0, has_side_effects=True),
    )(
        row_order,
        row_length,
        amplitude,
        row_order.reshape(1, lat_total),
        control,
        vertical,
        meridional,
        balance,
    )
    return pl.pallas_call(
        functools.partial(synthesis_kernel, per_peer),
        name="synthesis",
        out_shape=jax.ShapeDtypeStruct(control.shape, BF16),
        in_specs=[anywhere] * 4,
        out_specs=anywhere,
        scratch_shapes=[
            inputs[0],
            inputs[1],
            block,
            pltpu.VMEM((lat_total, SUBS, LANES), F32),
            pltpu.VMEM((levels, lons), BF16),
            table_vmem,
            pltpu.VMEM((levels, lons + LANES), F32),
            dma((11,)),
        ],
    )(row_order, row_length, balanced, basis)


def solution(mesh):
    return jax.shard_map(
        body,
        mesh=mesh,
        in_specs=(
            P("var", "lat", None, None),
            P(),
            P(),
            P("var", None, None),
            P("var", None),
            P("var", None, None),
            P("var", None, None),
        ),
        out_specs=P("var", "lat", None, None),
        check_vma=False,
    )
```
